32 devices in a mesh: groups: 2 (over y), dp: 2 (over core), tensor: 8 (over z, x).
Axes of the slice: x: 2, y: 2, z: 4, core: 2. Of those that a mesh axis runs over, the one named last changes fastest.
Arguments:
- tokens: bfloat16 [512, 8192], P(('groups', 'dp', 'tensor')), parts along dimension 0, may hold values from -134 to 134
- ln_gain: float32 [8192], replicated, may hold values from 0.25 to 1.75
- gate_weight: bfloat16 [8192, 16384], P('dp', 'tensor'), may hold values from -0.09375 to 0.09375
- up_weight: bfloat16 [8192, 16384], P('dp', 'tensor'), may hold values from -0.09375 to 0.09375
- down_weight: bfloat16 [16384, 8192], P('tensor', 'dp'), may hold values from -0.0625 to 0.0625
- gate_mask: int32 [64, 128], replicated, may hold values from 0 to 1, as said below
- up_mask: int32 [64, 128], replicated, may hold values from 0 to 1, as said below
- down_mask: int32 [128, 64], replicated, may hold values from 0 to 1, as said below
Outputs:
- mlp_out: bfloat16 [512, 8192], P(('groups', 'dp', 'tensor')), parts along dimension 0
The draws below stay inside these ranges and needn't reach their ends.
There are 2 independent parts, one for each index of `groups`. The reference program is written for one: setup_inputs(seed, part) draws one part's arguments, and reference() takes and returns one part's arrays. A program takes and returns all parts, laid end to end along the dimension named above; an argument that names none is the same for every part. Nothing has to cross between parts.
Inputs may be any that keep to these rules, and one draw needn't show every extreme that they name: `gate_mask`: in every block column, each of the 2 owners' runs of 32 consecutive block rows holds at least one and at most 24 ones; in some column every owner's run holds exactly 24. `up_mask`: as gate_mask. `down_mask`: in every block row, each of the 2 owners' runs of 32 consecutive block columns holds at least one and at most 24 ones; in some row every owner's run holds exactly 24.
All inputs are finite; a program needn't handle non-finite values.
Results may differ from the reference program's by a relative error of at most 0.0065.
Values may be sent and summed in bfloat16 or wider, within the bound.
A program may use at most 448 MiB of HBM per device.

```python
import math
import jax
import jax.numpy as jnp
from jax import lax

D = 8192
FF = 16384
BLK = 128
CAP = 24
TOKENS = 256
DB = 64
FB = 128
OWN_BLOCKS = 32


def draw_tokens(key, part):
    subkeys = jax.random.split(key, 3)
    row_scale = jnp.exp(jax.random.uniform(subkeys[0], (TOKENS, 1), jnp.float32, 0.0, math.log(10.0)))
    column_scale = jnp.exp(jax.random.uniform(subkeys[1], (1, D), jnp.float32, 0.0, math.log(10.0)))
    pattern = jnp.clip(jax.random.normal(subkeys[2], (TOKENS, D), jnp.float32), -4.0, 4.0)
    return (pattern * row_scale * column_scale / 3.0).astype(jnp.bfloat16)


def tile_mask(key, matrix_id):
    subkey = jax.random.fold_in(key, matrix_id)
    key_counts, key_fullest, key_scores = jax.random.split(subkey, 3)
    owners = DB // OWN_BLOCKS
    lowest = max(1, OWN_BLOCKS // 8)
    counts = jax.random.randint(key_counts, (owners, FB), lowest, CAP + 1)
    fullest = jax.random.randint(key_fullest, (), 0, FB)
    counts = jnp.where(jnp.arange(FB)[None, :] == fullest, CAP, counts)
    scores = jax.random.randint(key_scores, (owners, FB, OWN_BLOCKS), 0, 1 << 20) * OWN_BLOCKS
    scores = scores + jnp.arange(OWN_BLOCKS)[None, None, :]
    ranking = jnp.argsort(jnp.argsort(scores, axis=-1), axis=-1)
    return (ranking < counts[:, :, None]).astype(jnp.int32)


def draw_gate_mask(key, part):
    return tile_mask(key, 1).transpose(0, 2, 1).reshape(DB, FB)


def draw_up_mask(key, part):
    return tile_mask(key, 2).transpose(0, 2, 1).reshape(DB, FB)


def draw_down_mask(key, part):
    return tile_mask(key, 3).transpose(1, 0, 2).reshape(FB, DB)


def steps_of(key, shape, cuts, smallest, top_value):
    loudness = 1.0
    for position, shards_of in cuts:
        steps = jax.random.uniform(jax.random.fold_in(jax.random.fold_in(key, 6), position), (shards_of,), jnp.float32, smallest / len(cuts), top_value / len(cuts))
        loudness = loudness * jnp.repeat(jnp.exp(steps), shape[position] // shards_of).reshape((-1,) + (1,) * (len(shape) - 1 - position))
    return loudness


def normal_values(key, extent, spread, reach, pieces=(), held_as=jnp.bfloat16):
    array = spread * jax.random.normal(key, extent, jnp.float32)
    if pieces:
        array = array * steps_of(key, extent, pieces, -0.22, 0.18)
    return jnp.clip(array, -reach, reach).astype(held_as)


def setup_inputs(seed: int = 0, part: int = 0) -> dict:
    seeds = jax.random.split(jax.random.key(seed), 9)
    part_keys = jax.random.split(jax.random.fold_in(seeds[8], part), 9)
    return {
        "tokens": draw_tokens(jax.random.fold_in(jax.random.fold_in(seeds[8], part), 71), part),
        "ln_gain": jnp.clip(1.0 + 0.15 * jax.random.normal(seeds[1], (D,), jnp.float32), 0.25, 1.75),
        "gate_weight": normal_values(seeds[2], (D, FF), (D // 2) ** -0.5, 0.09375, ((0, 2), (1, 8))),
        "up_weight": normal_values(seeds[3], (D, FF), (D // 2) ** -0.5, 0.09375, ((0, 2), (1, 8))),
        "down_weight": normal_values(seeds[4], (FF, D), (FF // 2) ** -0.5, 0.0625, ((0, 8), (1, 2))),
        "gate_mask": draw_gate_mask(jax.random.fold_in(seeds[8], 71), part),
        "up_mask": draw_up_mask(jax.random.fold_in(seeds[8], 71), part),
        "down_mask": draw_down_mask(jax.random.fold_in(seeds[8], 71), part),
    }


def masked_weight(weight, block_mask):
    row_blocks, column_blocks = block_mask.shape
    tiled_weight = weight.reshape(row_blocks, BLK, column_blocks, BLK) * block_mask[:, None, :, None].astype(weight.dtype)
    return tiled_weight.reshape(row_blocks * BLK, column_blocks * BLK)

def reference(tokens, ln_gain, gate_weight, up_weight, down_weight, gate_mask, up_mask, down_mask):
    values = tokens.astype(jnp.float32)
    average = lax.optimization_barrier(jnp.mean(values, axis=1, keepdims=True))
    centered = values - average
    variance = lax.optimization_barrier(jnp.mean(centered * centered, axis=1, keepdims=True))
    normed = (centered * jax.lax.rsqrt(variance + 1e-05) * ln_gain).astype(jnp.bfloat16)
    gate_sums = jnp.dot(normed, masked_weight(gate_weight, gate_mask), preferred_element_type=jnp.float32)
    up_sums = jnp.dot(normed, masked_weight(up_weight, up_mask), preferred_element_type=jnp.float32)
    hidden = (jax.nn.silu(gate_sums) * up_sums).astype(jnp.bfloat16)
    mlp_out = jnp.dot(hidden, masked_weight(down_weight, down_mask), preferred_element_type=jnp.float32)
    return mlp_out.astype(jnp.bfloat16)
```

```python
import functools

import jax
import jax.numpy as jnp
from jax import lax
from jax.experimental import pallas as pl
from jax.experimental.pallas import tpu as pltpu
from jax.sharding import PartitionSpec as P

BLK = 128
ROWS = 16
DNC = 512
AG0 = (16, 16)
AG1 = (16, 8)
GRP = 512
DCH = 1024
EPSILON = 1e-05
F32 = jnp.float32
BF16 = jnp.bfloat16


def layer_norm(tokens, ln_gain):
    values = tokens.astype(F32)
    average = jnp.mean(values, axis=1, keepdims=True)
    centered = values - average
    variance = jnp.mean(centered * centered, axis=1, keepdims=True)
    return (centered * lax.rsqrt(variance + EPSILON) * ln_gain).astype(BF16)


def expand(mask, dtype):
    return jnp.repeat(jnp.repeat(mask.astype(dtype), BLK, axis=0), BLK, axis=1)


def general(tokens, ln_gain, gate_weight, up_weight, down_weight, gate_mask, up_mask, down_mask):
    t = lax.axis_index("tensor")
    d = lax.axis_index("dp")
    kl, fl = gate_weight.shape
    kb, fb = kl // BLK, fl // BLK
    normed = layer_norm(tokens, ln_gain)
    rows = lax.all_gather(normed, ("dp", "tensor"), axis=0, tiled=True)
    mine = lax.dynamic_slice_in_dim(rows, d * kl, kl, 1)

    def cut(mask, r0, c0, nr, nc):
        return expand(lax.dynamic_slice(mask, (r0, c0), (nr, nc)), BF16)

    gw = gate_weight * cut(gate_mask, d * kb, t * fb, kb, fb)
    uw = up_weight * cut(up_mask, d * kb, t * fb, kb, fb)
    dw = down_weight * cut(down_mask, t * fb, d * kb, fb, kb)
    gate = lax.psum(jnp.dot(mine, gw, preferred_element_type=F32), "dp")
    up = lax.psum(jnp.dot(mine, uw, preferred_element_type=F32), "dp")
    hidden = (jax.nn.silu(gate) * up).astype(BF16)
    part = jnp.dot(hidden, dw, preferred_element_type=F32)
    full = lax.all_gather(part, "dp", axis=1, tiled=True)
    half = full.shape[0] // lax.axis_size("dp")
    full = lax.dynamic_slice_in_dim(full, d * half, half, 0)
    return lax.psum_scatter(full, "tensor", scatter_dimension=0, tiled=True).astype(BF16)


def fused_kernel(
    Z,
    gm, um, dmt, tok, gain, gw_hbm, uw_hbm, dw_hbm,
    out,
    gu, dw, nrm, xbuf, exs, exr, own, hid, sb, acc, rx, rlin, zr, fin, finrx,
    w_sem, in_s, in_r, agz_s, agz_r, agl_s, agx_s, agx_r, ago_s, ago_r,
    ae_s, ae_r, aez_s, aez_r, ael_s, ex_s, ex_r, hd_s, hd_r,
    rx_s, rx_r, rz_s, rz_r, rl_s, rl_r, fn_s, fn_r,
):
    kl, fl = gu.shape[1:]
    half = fl // 2
    line = Z * ROWS
    groups = half // GRP
    chunks = kl // DCH
    d = lax.axis_index("dp")
    t = lax.axis_index("tensor")
    z = t // 2
    x = t % 2
    peer = {"dp": 1 - d}
    xnbr = {"tensor": z * 2 + (1 - x)}
    outer = jnp.logical_or(z == 0, z == Z - 1)
    inner = jnp.logical_not(outer)

    def zx(i):
        hi, lo = z // 2, z % 2
        if i & 2:
            hi = 1 - hi
        if i & 1:
            lo = 1 - lo
        return hi * 2 + lo

    def zdev(i):
        return {"tensor": zx(i) * 2 + x}

    def slot(j):
        return pl.ds(pl.multiple_of(j * ROWS, ROWS), ROWS)

    def remote(src, dst, ss, rs, dev):
        return pltpu.make_async_remote_copy(
            src_ref=src, dst_ref=dst, send_sem=ss, recv_sem=rs,
            device_id=dev, device_id_type=pl.DeviceIdType.MESH,
        )

    def wcopy(k):
        which, part = k // 4, k % 4
        src, dst = ((gw_hbm, gu.at[0]), (uw_hbm, gu.at[1]), (dw_hbm, dw))[which]
        n = src.shape[0] // 4
        return pltpu.make_async_copy(
            src.at[pl.ds(part * n, n), :], dst.at[pl.ds(part * n, n), :], w_sem.at[k]
        )

    barrier = pltpu.get_barrier_semaphore()

    def greet(dev):
        pl.semaphore_signal(barrier, inc=1, device_id=dev, device_id_type=pl.DeviceIdType.MESH)

    greet(peer)
    greet(xnbr)
    greet(zdev(1))
    greet(zdev(2))

    @pl.when(inner)
    def _():
        greet(zdev(3))

    for k in range(12):
        wcopy(k).start()

    values = tok[...].astype(F32)
    average = jnp.mean(values, axis=1, keepdims=True)
    centered = values - average
    variance = jnp.mean(centered * centered, axis=1, keepdims=True)
    nrm[...] = (centered * lax.rsqrt(variance + EPSILON) * gain[...]).astype(BF16)

    @pl.when(inner)
    def _():
        pl.semaphore_wait(barrier, 5)

    @pl.when(outer)
    def _():
        pl.semaphore_wait(barrier, 4)

    def cols(o):
        return pl.ds(pl.multiple_of(o * kl, kl), kl)

    first = remote(nrm.at[:, cols(1 - d)], xbuf.at[d, slot(z), :], in_s, in_r, peer)
    first.start()
    xbuf[d, slot(z), :] = nrm[:, cols(d)]
    remote(nrm.at[:, cols(d)], xbuf.at[1 - d, slot(z), :], in_s, in_r, peer).wait_recv()

    cuts = []
    for widths in (AG0, AG1):
        at, spans = 0, []
        for w in widths:
            spans.append(pl.ds(at * BLK, w * BLK))
            at += w
        cuts.append(spans)
    main1 = sum(AG1) * BLK
    ecols = pl.ds(main1, kl - main1)

    def agz(h, c, i):
        b = xbuf.at[h, slot(z), cuts[h][c]]
        return remote(b, b, agz_s.at[h, c, i - 1], agz_r.at[h, c, i - 1], zdev(i))

    def agz_in(h, c, i):
        b = xbuf.at[h, slot(zx(i)), cuts[h][c]]
        return remote(b, b, agz_s.at[h, c, i - 1], agz_r.at[h, c, i - 1], zdev(i))

    def agl(h, c):
        b = xbuf.at[h, slot(zx(2)), cuts[h][c]]
        return remote(b, b, agl_s.at[h, c], agz_r.at[h, c, 2], zdev(1))

    def agx(h, c, i):
        return remote(xbuf.at[h, slot(zx(i)), cuts[h][c]], xbuf.at[h, slot(Z + zx(i)), cuts[h][c]],
                      agx_s.at[h, c, i - 1], agx_r.at[h, c, i - 1], xnbr)

    def ago(h):
        span = pl.ds(0, main1 if h else kl)
        return remote(xbuf.at[h, slot(z), span], xbuf.at[h, slot(Z + z), span],
                      ago_s.at[h], ago_r.at[h], xnbr)

    def age():
        return remote(xbuf.at[1, slot(z), ecols], xbuf.at[1, slot(Z + z), ecols], ae_s, ae_r, xnbr)

    def aez(k, i):
        b = xbuf.at[1, slot(k * Z + z), ecols]
        return remote(b, b, aez_s.at[k, i - 1], aez_r.at[k, i - 1], zdev(i))

    def aez_in(k, i):
        b = xbuf.at[1, slot(k * Z + zx(i)), ecols]
        return remote(b, b, aez_s.at[k, i - 1], aez_r.at[k, i - 1], zdev(i))

    def ael(k):
        b = xbuf.at[1, slot(k * Z + zx(2)), ecols]
        return remote(b, b, ael_s.at[k], aez_r.at[k, 2], zdev(1))

    def ag_send(h, c):
        agz(h, c, 2).start()
        agz(h, c, 1).start()

        @pl.when(inner)
        def _():
            agz(h, c, 3).start()

    def ag_forward(h, c):
        agz_in(h, c, 2).wait_recv()

        @pl.when(inner)
        def _():
            agl(h, c).start()

        agx(h, c, 2).start()
        for i in (1, 3):
            agz_in(h, c, i).wait_recv()
            agx(h, c, i).start()

    def ag_edge_send():
        age().wait_recv()
        for k in range(2):
            aez(k, 2).start()
            aez(k, 1).start()

            @pl.when(inner)
            def _():
                aez(k, 3).start()

    def ag_edge_forward():
        for k in range(2):
            aez_in(k, 2).wait_recv()

            @pl.when(inner)
            def _():
                ael(k).start()

    def ag_finish(h):
        ago(h).wait_recv()
        for c in range(len(cuts[h])):
            for i in (1, 2, 3):
                agx(h, c, i).wait_recv()
        if h:
            for k in range(2):
                aez_in(k, 1).wait_recv()
                aez_in(k, 3).wait_recv()

    def ag_drain():
        age().wait_send()
        for k in range(2):
            aez(k, 1).wait_send()
            aez(k, 2).wait_send()

            @pl.when(inner)
            def _():
                aez(k, 3).wait_send()
                ael(k).wait_send()

        for h in range(2):
            ago(h).wait_send()
            for c in range(len(cuts[h])):
                for i in (1, 2, 3):
                    agx(h, c, i).wait_send()
                agz(h, c, 1).wait_send()
                agz(h, c, 2).wait_send()

                @pl.when(inner)
                def _():
                    agz(h, c, 3).wait_send()
                    agl(h, c).wait_send()

    def prune(k):
        wcopy(k).wait()
        which, part = k // 4, k % 4
        w = (gu.at[0], gu.at[1], dw)[which]
        nr, nc = w.shape[0] // BLK, w.shape[1] // BLK
        n = nr // 4

        def body(b, carry):
            rb = part * n + b
            rows = pl.ds(pl.multiple_of(rb * BLK, BLK), BLK)
            for cb in range(nc):
                if which == 2:
                    bit = dmt[d * nc + cb, t * nr + rb]
                else:
                    bit = (gm, um)[which][d * nr + rb, t * nc + cb]
                keep = jnp.full((16, BLK), bit.astype(F32), F32).astype(BF16)
                tile = w[rows, cb * BLK:(cb + 1) * BLK].reshape(BLK // 16, 16, BLK)
                w[rows, cb * BLK:(cb + 1) * BLK] = (tile * keep[None]).reshape(BLK, BLK)
            return carry

        lax.fori_loop(0, n, body, 0)

    def ex(h, q):
        return remote(exs.at[q], exr.at[q], ex_s.at[h, q], ex_r.at[h, q], peer)

    def group(h, q, mine):
        cs = pl.ds(pl.multiple_of((d if mine else 1 - d) * half + q * GRP, GRP), GRP)

        def body(m, carry):
            p = jnp.dot(xbuf[h], gu[m, :, cs], preferred_element_type=F32)
            if mine:
                own[q, m] = p
            else:
                exs[q, m] = p.astype(BF16)
            return carry

        lax.fori_loop(0, 2, body, 0)
        if not mine:
            ex(h, q).start()

    def hcols(o, q):
        return pl.ds(pl.multiple_of(o * half + q * GRP, GRP), GRP)

    def hd(h, q, o):
        blk = hid.at[:, hcols(o, q)]
        return remote(blk, blk, hd_s.at[h, q], hd_r.at[h, q], peer)

    def hidden(h, q):
        ex(h, q).wait()
        g = own[q, 0] + exr[q, 0].astype(F32)
        u = own[q, 1] + exr[q, 1].astype(F32)
        hid[:, hcols(d, q)] = (g / (1.0 + jnp.exp(-g)) * u).astype(BF16)
        hd(h, q, d).start()

    def chunk(c):
        return pl.ds(c * DCH, DCH)

    def rsx(h, c, i):
        return remote(sb.at[h, slot(Z + zx(i)), chunk(c)], rx.at[h, slot(zx(i)), chunk(c)],
                      rx_s.at[h, c, i], rx_r.at[h, c, i], xnbr)

    def rsz(h, c, i):
        return remote(sb.at[h, slot(zx(i)), chunk(c)], zr.at[h, i - 1, :, chunk(c)],
                      rz_s.at[h, c, i - 1], rz_r.at[h, c, i - 1], zdev(i))

    def rsl(h, c):
        return remote(sb.at[h, slot(zx(3)), chunk(c)], rlin.at[h, :, chunk(c)],
                      rl_s.at[h, c], rl_r.at[h, c], zdev(1))

    def down(h, c):
        def body(j, carry):
            cs = pl.ds(pl.multiple_of(c * DCH + j * DNC, DNC), DNC)
            p = jnp.dot(hid[...], dw[:, cs], preferred_element_type=F32)
            acc[h, :, cs] = p[:line]
            sb[h, line:, cs] = p[line:].astype(BF16)
            return carry

        lax.fori_loop(0, DCH // DNC, body, 0)
        for i in (3, 2, 1, 0):
            rsx(h, c, i).start()

    def merge(h, c, i):
        rsx(h, c, i).wait_recv()
        return acc[h, slot(zx(i)), chunk(c)] + rx[h, slot(zx(i)), chunk(c)].astype(F32)

    def rs_send(h, c):
        sb[h, slot(zx(3)), chunk(c)] = merge(h, c, 3).astype(BF16)

        @pl.when(outer)
        def _():
            rsl(h, c).start()

        @pl.when(inner)
        def _():
            rsz(h, c, 3).start()

        total = merge(h, c, 2)

        @pl.when(outer)
        def _():
            sb[h, slot(zx(2)), chunk(c)] = total.astype(BF16)
            rsz(h, c, 2).start()

        sb[h, slot(zx(1)), chunk(c)] = merge(h, c, 1).astype(BF16)
        rsz(h, c, 1).start()

    def rs_relay(h, c):
        @pl.when(inner)
        def _():
            rsl(h, c).wait_recv()
            total = acc[h, slot(zx(2)), chunk(c)] + rx[h, slot(zx(2)), chunk(c)].astype(F32)
            sb[h, slot(zx(2)), chunk(c)] = (total + rlin[h, :, chunk(c)].astype(F32)).astype(BF16)
            rsz(h, c, 2).start()

    def last(c):
        return remote(fin.at[:, chunk(c)], finrx.at[:, chunk(c)], fn_s.at[c], fn_r.at[c], peer)

    def rs_final(h, c):
        rsz(h, c, 1).wait_recv()
        rsz(h, c, 2).wait_recv()

        @pl.when(inner)
        def _():
            rsz(h, c, 3).wait_recv()

        total = merge(h, c, 0)
        for i in range(3):
            total = total + zr[h, i, :, chunk(c)].astype(F32)
        result = total.astype(BF16)

        @pl.when(d == h)
        def _():
            out[:, pl.ds(pl.multiple_of(d * kl + c * DCH, DCH), DCH)] = result

        @pl.when(d != h)
        def _():
            fin[:, chunk(c)] = result
            last(c).start()

    def rs_drain(h):
        for c in range(chunks):
            for i in range(4):
                rsx(h, c, i).wait_send()
            rsz(h, c, 1).wait_send()
            rsz(h, c, 2).wait_send()

            @pl.when(outer)
            def _():
                rsl(h, c).wait_send()

            @pl.when(inner)
            def _():
                rsz(h, c, 3).wait_send()

    n0, n1 = len(AG0), len(AG1)
    for c in range(n0):
        ag_send(0, c)
    ago(0).start()
    age().start()
    ago(1).start()

    @pl.when(outer)
    def _():
        zr[:, 2] = jnp.zeros_like(zr[:, 2])

    order = [0, 4, 1, 5, 2, 6, 3, 7, 8, 9, 10, 11]
    for k in order[:3]:
        prune(k)
    order = order[3:]
    for c in range(n0):
        ag_forward(0, c)
        if c < n1:
            ag_send(1, c)
        for k in order[:2]:
            prune(k)
        order = order[2:]
    for c in range(n0, n1):
        ag_send(1, c)
    ag_edge_send()
    for k in order:
        prune(k)
    ag_finish(0)
    group(0, 0, False)
    ag_forward(1, 0)
    group(0, 1, False)
    for c in range(1, n1):
        ag_forward(1, c)
    group(0, 0, True)
    hidden(0, 0)
    ag_edge_forward()
    group(0, 1, True)
    hidden(0, 1)
    for q in range(groups):
        hd(0, q, 1 - d).wait_recv()
    for c in range(chunks):
        down(0, c)
    for q in range(groups):
        hd(0, q, d).wait_send()
    ag_finish(1)
    group(1, 0, False)
    group(1, 1, False)
    rs_send(0, 0)
    group(1, 0, True)
    rs_send(0, 1)
    rs_relay(0, 0)
    hidden(1, 0)
    group(1, 1, True)
    hidden(1, 1)
    rs_send(0, 2)
    rs_relay(0, 1)
    for q in range(groups):
        hd(1, q, 1 - d).wait_recv()
    down(1, 0)
    rs_send(0, 3)
    rs_relay(0, 2)
    down(1, 1)
    rs_relay(0, 3)
    down(1, 2)
    rs_send(1, 0)
    down(1, 3)
    for q in range(groups):
        hd(1, q, d).wait_send()
    for c in range(chunks):
        rs_final(0, c)
    rs_send(1, 1)
    rs_relay(1, 0)
    rs_send(1, 2)
    rs_relay(1, 1)
    rs_send(1, 3)
    for c in range(2, chunks):
        rs_relay(1, c)
    for c in range(chunks):
        rs_final(1, c)
    first.wait_send()
    ag_drain()
    rs_drain(0)
    rs_drain(1)
    for c in range(chunks):
        last(c).wait()
    out[:, cols(1 - d)] = finrx[...]


def fused(Z, tokens, ln_gain, gate_weight, up_weight, down_weight, gate_mask, up_mask, down_mask):
    kl, fl = gate_weight.shape
    dim = tokens.shape[1]
    half = fl // 2
    groups = half // GRP
    chunks = kl // DCH
    line = Z * ROWS
    m = 2 * line
    cuts = max(len(AG0), len(AG1))
    dma = pltpu.SemaphoreType.DMA
    vm = pl.BlockSpec(memory_space=pltpu.VMEM)
    sm = pl.BlockSpec(memory_space=pltpu.SMEM)
    hbm = pl.BlockSpec(memory_space=pl.ANY)
    flops = 2 * 2 * m * kl * fl * 3
    return pl.pallas_call(
        functools.partial(fused_kernel, Z),
        out_shape=jax.ShapeDtypeStruct((ROWS, dim), BF16),
        in_specs=[sm, sm, sm, vm, vm, hbm, hbm, hbm],
        out_specs=vm,
        scratch_shapes=[
            pltpu.VMEM((2, kl, fl), BF16),
            pltpu.VMEM((fl, kl), BF16),
            pltpu.VMEM((ROWS, dim), BF16),
            pltpu.VMEM((2, m, kl), BF16),
            pltpu.VMEM((groups, 2, m, GRP), BF16),
            pltpu.VMEM((groups, 2, m, GRP), BF16),
            pltpu.VMEM((groups, 2, m, GRP), F32),
            pltpu.VMEM((m, fl), BF16),
            pltpu.VMEM((2, m, kl), BF16),
            pltpu.VMEM((2, line, kl), F32),
            pltpu.VMEM((2, line, kl), BF16),
            pltpu.VMEM((2, ROWS, kl), BF16),
            pltpu.VMEM((2, 3, ROWS, kl), BF16),
            pltpu.VMEM((ROWS, kl), BF16),
            pltpu.VMEM((ROWS, kl), BF16),
            dma((12,)),
            dma, dma,
            dma((2, cuts, 3)), dma((2, cuts, 3)), dma((2, cuts)),
            dma((2, cuts, 3)), dma((2, cuts, 3)),
            dma((2,)), dma((2,)),
            dma, dma, dma((2, 3)), dma((2, 3)), dma((2,)),
            dma((2, groups)), dma((2, groups)),
            dma((2, groups)), dma((2, groups)),
            dma((2, chunks, 4)), dma((2, chunks, 4)),
            dma((2, chunks, 3)), dma((2, chunks, 3)),
            dma((2, chunks)), dma((2, chunks)),
            dma((chunks,)), dma((chunks,)),
        ],
        compiler_params=pltpu.CompilerParams(
            collective_id=0, has_side_effects=True, vmem_limit_bytes=63 * 1024 * 1024
        ),
        cost_estimate=pl.CostEstimate(
            flops=flops, bytes_accessed=6 * kl * fl, transcendentals=0
        ),
    )(gate_mask, up_mask, down_mask.T, tokens, ln_gain.reshape(1, dim),
      gate_weight, up_weight, down_weight)


def solution(mesh):
    tensor = mesh.shape["tensor"]
    owners = mesh.shape["dp"]
    copies = mesh.shape["groups"]
    Z = tensor // 2

    def per_device(tokens, ln_gain, gate_weight, *rest):
        rows = tokens.shape[0]
        kl, fl = gate_weight.shape
        fits = (
            owners == 2 and tensor == 2 * Z and rows == ROWS and Z == 4
            and kl == 4 * DCH and fl == 4 * GRP
        )
        if fits:
            return fused(Z, tokens, ln_gain, gate_weight, *rest)
        return general(tokens, ln_gain, gate_weight, *rest)

    in_specs = (
        P(("groups", "dp", "tensor"), None),
        P(),
        P("dp", "tensor"),
        P("dp", "tensor"),
        P("tensor", "dp"),
        P(),
        P(),
        P(),
    )
    out_specs = P(("groups", "dp", "tensor"), None)
    return jax.shard_map(
        per_device, mesh=mesh, in_specs=in_specs, out_specs=out_specs, check_vma=False
    )
```

```python
import functools

import jax
import jax.numpy as jnp
from jax import lax
from jax.experimental import pallas as pl
from jax.experimental.pallas import tpu as pltpu
from jax.sharding import PartitionSpec as P

BLK = 128
ROWS = 16
DNC = 512
PW = 4
EARLY = 2
DIRECT = ((0, 0), (0, 1), (0, 2), (0, 3), (1, 0), (1, 1), (1, 2), (1, 3))
LOADS = (0, 4, 1, 5, 2, 6, 3, 7, 8, 9, 10, 11)
AG0 = (16, 16)
AG1 = (16, 8)
GRP = 512
DCH = 1024
EPSILON = 1e-05
F32 = jnp.float32
BF16 = jnp.bfloat16


def layer_norm(tokens, ln_gain):
    values = tokens.astype(F32)
    average = jnp.mean(values, axis=1, keepdims=True)
    centered = values - average
    variance = jnp.mean(centered * centered, axis=1, keepdims=True)
    return (centered * lax.rsqrt(variance + EPSILON) * ln_gain).astype(BF16)


def expand(mask, dtype):
    return jnp.repeat(jnp.repeat(mask.astype(dtype), BLK, axis=0), BLK, axis=1)


def general(tokens, ln_gain, gate_weight, up_weight, down_weight, gate_mask, up_mask, down_mask):
    t = lax.axis_index("tensor")
    d = lax.axis_index("dp")
    kl, fl = gate_weight.shape
    kb, fb = kl // BLK, fl // BLK
    normed = layer_norm(tokens, ln_gain)
    rows = lax.all_gather(normed, ("dp", "tensor"), axis=0, tiled=True)
    mine = lax.dynamic_slice_in_dim(rows, d * kl, kl, 1)

    def cut(mask, r0, c0, nr, nc):
        return expand(lax.dynamic_slice(mask, (r0, c0), (nr, nc)), BF16)

    gw = gate_weight * cut(gate_mask, d * kb, t * fb, kb, fb)
    uw = up_weight * cut(up_mask, d * kb, t * fb, kb, fb)
    dw = down_weight * cut(down_mask, t * fb, d * kb, fb, kb)
    gate = lax.psum(jnp.dot(mine, gw, preferred_element_type=F32), "dp")
    up = lax.psum(jnp.dot(mine, uw, preferred_element_type=F32), "dp")
    hidden = (jax.nn.silu(gate) * up).astype(BF16)
    part = jnp.dot(hidden, dw, preferred_element_type=F32)
    full = lax.all_gather(part, "dp", axis=1, tiled=True)
    half = full.shape[0] // lax.axis_size("dp")
    full = lax.dynamic_slice_in_dim(full, d * half, half, 0)
    return lax.psum_scatter(full, "tensor", scatter_dimension=0, tiled=True).astype(BF16)


def fused_kernel(
    Z,
    gm_hbm, um_hbm, dm_hbm, tok_hbm, gain_hbm, gw_hbm, uw_hbm, dw_hbm,
    out,
    gm, um, dmt, tok, gain,
    gu, dw, nrm, xbuf, exs, exr, own, pre, hid, sb, acc, rx, rlin, zr, fin, finrx,
    o_sem, w_sem, in_s, in_r, agz_s, agz_r, agl_s, agx_s, agx_r, ago_s, ago_r,
    ae_s, ae_r, aez_s, aez_r, ael_s, ex_s, ex_r, hd_s, hd_r,
    rx_s, rx_r, rz_s, rz_r, rl_s, rl_r, fn_s, fn_r,
):
    kl, fl = gu.shape[1:]
    half = fl // 2
    line = Z * ROWS
    groups = half // GRP
    chunks = kl // DCH
    d = lax.axis_index("dp")
    t = lax.axis_index("tensor")
    z = t // 2
    x = t % 2
    peer = {"dp": 1 - d}
    xnbr = {"tensor": z * 2 + (1 - x)}
    outer = jnp.logical_or(z == 0, z == Z - 1)
    inner = jnp.logical_not(outer)

    def zx(i):
        hi, lo = z // 2, z % 2
        if i & 2:
            hi = 1 - hi
        if i & 1:
            lo = 1 - lo
        return hi * 2 + lo

    def zdev(i):
        return {"tensor": zx(i) * 2 + x}

    def slot(j):
        return pl.ds(pl.multiple_of(j * ROWS, ROWS), ROWS)

    def remote(src, dst, ss, rs, dev):
        return pltpu.make_async_remote_copy(
            src_ref=src, dst_ref=dst, send_sem=ss, recv_sem=rs,
            device_id=dev, device_id_type=pl.DeviceIdType.MESH,
        )

    def wcopy(k):
        which, part = k // 4, k % 4
        src, dst = ((gw_hbm, gu.at[0]), (uw_hbm, gu.at[1]), (dw_hbm, dw))[which]
        n = src.shape[0] // 4
        return pltpu.make_async_copy(
            src.at[pl.ds(part * n, n), :], dst.at[pl.ds(part * n, n), :], w_sem.at[k]
        )

    barrier = pltpu.get_barrier_semaphore()

    def greet(dev):
        pl.semaphore_signal(barrier, inc=1, device_id=dev, device_id_type=pl.DeviceIdType.MESH)

    greet(peer)
    greet(xnbr)
    greet(zdev(1))
    greet(zdev(2))
    greet(zdev(3))

    kb = kl // BLK
    mine = pl.ds(pl.multiple_of(d * kb, kb), kb)
    small = [
        pltpu.make_async_copy(src, dst, o_sem.at[n])
        for n, (src, dst) in enumerate((
            (tok_hbm, tok), (gain_hbm, gain),
            (gm_hbm.at[mine, :], gm), (um_hbm.at[mine, :], um), (dm_hbm.at[mine, :], dmt),
        ))
    ]
    for copy in small:
        copy.start()
    small[0].wait()
    for copy in small[1:]:
        copy.wait()
    for k in LOADS:
        wcopy(k).start()

    values = tok[...].astype(F32)
    average = jnp.mean(values, axis=1, keepdims=True)
    centered = values - average
    variance = jnp.mean(centered * centered, axis=1, keepdims=True)
    nrm[...] = (centered * lax.rsqrt(variance + EPSILON) * gain[...]).astype(BF16)

    pl.semaphore_wait(barrier, 5)

    def cols(o):
        return pl.ds(pl.multiple_of(o * kl, kl), kl)

    first = remote(nrm.at[:, cols(1 - d)], xbuf.at[d, slot(z), :], in_s, in_r, peer)
    first.start()
    xbuf[d, slot(z), :] = nrm[:, cols(d)]
    remote(nrm.at[:, cols(d)], xbuf.at[1 - d, slot(z), :], in_s, in_r, peer).wait_recv()

    cuts = []
    for widths in (AG0, AG1):
        at, spans = 0, []
        for w in widths:
            spans.append(pl.ds(at * BLK, w * BLK))
            at += w
        cuts.append(spans)
    main1 = sum(AG1) * BLK
    ecols = pl.ds(main1, kl - main1)

    def agz(h, c, i):
        b = xbuf.at[h, slot(z), cuts[h][c]]
        return remote(b, b, agz_s.at[h, c, i - 1], agz_r.at[h, c, i - 1], zdev(i))

    def agz_in(h, c, i):
        b = xbuf.at[h, slot(zx(i)), cuts[h][c]]
        return remote(b, b, agz_s.at[h, c, i - 1], agz_r.at[h, c, i - 1], zdev(i))

    def agl(h, c):
        b = xbuf.at[h, slot(zx(2)), cuts[h][c]]
        return remote(b, b, agl_s.at[h, c], agz_r.at[h, c, 2], zdev(1))

    def agx(h, c, i):
        return remote(xbuf.at[h, slot(zx(i)), cuts[h][c]], xbuf.at[h, slot(Z + zx(i)), cuts[h][c]],
                      agx_s.at[h, c, i - 1], agx_r.at[h, c, i - 1], xnbr)

    def ago(h):
        span = pl.ds(0, main1 if h else kl)
        return remote(xbuf.at[h, slot(z), span], xbuf.at[h, slot(Z + z), span],
                      ago_s.at[h], ago_r.at[h], xnbr)

    def age():
        return remote(xbuf.at[1, slot(z), ecols], xbuf.at[1, slot(Z + z), ecols], ae_s, ae_r, xnbr)

    def aez(k, i):
        b = xbuf.at[1, slot(k * Z + z), ecols]
        return remote(b, b, aez_s.at[k, i - 1], aez_r.at[k, i - 1], zdev(i))

    def aez_in(k, i):
        b = xbuf.at[1, slot(k * Z + zx(i)), ecols]
        return remote(b, b, aez_s.at[k, i - 1], aez_r.at[k, i - 1], zdev(i))

    def ael(k):
        b = xbuf.at[1, slot(k * Z + zx(2)), ecols]
        return remote(b, b, ael_s.at[k], aez_r.at[k, 2], zdev(1))

    def ag_send(h, c):
        agz(h, c, 2).start()
        agz(h, c, 1).start()

        @pl.when(inner)
        def _():
            agz(h, c, 3).start()

    def ag_forward(h, c):
        agz_in(h, c, 2).wait_recv()

        @pl.when(inner)
        def _():
            agl(h, c).start()

        agx(h, c, 2).start()
        for i in (1, 3):
            agz_in(h, c, i).wait_recv()
            agx(h, c, i).start()

    def ag_edge_send():
        age().wait_recv()
        for k in range(2):
            aez(k, 2).start()
            aez(k, 1).start()

            @pl.when(inner)
            def _():
                aez(k, 3).start()

    def ag_edge_forward():
        for k in range(2):
            aez_in(k, 2).wait_recv()

            @pl.when(inner)
            def _():
                ael(k).start()

    def ag_part(c):
        for i in (1, 2, 3):
            agx(0, c, i).wait_recv()

    def ag_finish(h):
        if h:
            ago(h).wait_recv()
        for c in range(0 if h else 1, len(cuts[h])):
            for i in (1, 2, 3):
                agx(h, c, i).wait_recv()
        if h:
            for k in range(2):
                aez_in(k, 1).wait_recv()
                aez_in(k, 3).wait_recv()

    def ag_drain():
        age().wait_send()
        for k in range(2):
            aez(k, 1).wait_send()
            aez(k, 2).wait_send()

            @pl.when(inner)
            def _():
                aez(k, 3).wait_send()
                ael(k).wait_send()

        for h in range(2):
            ago(h).wait_send()
            for c in range(len(cuts[h])):
                for i in (1, 2, 3):
                    agx(h, c, i).wait_send()
                agz(h, c, 1).wait_send()
                agz(h, c, 2).wait_send()

                @pl.when(inner)
                def _():
                    agz(h, c, 3).wait_send()
                    agl(h, c).wait_send()

    def prune(k):
        wcopy(k).wait()
        which, part = k // 4, k % 4
        w = (gu.at[0], gu.at[1], dw)[which]
        nr, nc = w.shape[0] // BLK, w.shape[1] // BLK
        n = nr // 4

        def body(b, carry):
            rb = part * n + b
            rows = pl.ds(pl.multiple_of(rb * BLK, BLK), BLK)
            for c0 in range(0, nc, PW):
                keep = []
                for cb in range(c0, c0 + PW):
                    if which == 2:
                        bit = dmt[cb, t * nr + rb]
                    else:
                        bit = (gm, um)[which][rb, t * nc + cb]
                    keep.append(jnp.full((16, BLK), bit.astype(F32), F32).astype(BF16))
                keep = jnp.concatenate(keep, axis=1)
                cs = slice(c0 * BLK, (c0 + PW) * BLK)
                tile = w[rows, cs].reshape(BLK // 16, 16, PW * BLK)
                w[rows, cs] = (tile * keep[None]).reshape(BLK, PW * BLK)
            return carry

        lax.fori_loop(0, n, body, 0)

    def ex(h, q):
        return remote(exs.at[q], exr.at[q], ex_s.at[h, q], ex_r.at[h, q], peer)

    def group(h, q, mine, part=None):
        cs = pl.ds(pl.multiple_of((d if mine else 1 - d) * half + q * GRP, GRP), GRP)
        cut = AG0[0] * BLK
        ks = {None: pl.ds(0, kl), 0: pl.ds(0, cut), 1: pl.ds(cut, kl - cut)}[part]

        def body(m, carry):
            p = jnp.dot(xbuf[h, :, ks], gu[m, ks, cs], preferred_element_type=F32)
            if part == 1:
                p = p + (own[q, m] if mine else pre[q * 2 + m])
            if mine:
                own[q, m] = p
            elif part == 0:
                pre[q * 2 + m] = p
            else:
                exs[q, m] = p.astype(BF16)
            return carry

        lax.fori_loop(0, 2, body, 0)
        if not mine and part != 0:
            ex(h, q).start()

    def hcols(o, q):
        return pl.ds(pl.multiple_of(o * half + q * GRP, GRP), GRP)

    def hd(h, q, o):
        blk = hid.at[:, hcols(o, q)]
        return remote(blk, blk, hd_s.at[h, q], hd_r.at[h, q], peer)

    def hidden(h, q):
        ex(h, q).wait()
        g = own[q, 0] + exr[q, 0].astype(F32)
        u = own[q, 1] + exr[q, 1].astype(F32)
        hid[:, hcols(d, q)] = (g / (1.0 + jnp.exp(-g)) * u).astype(BF16)
        hd(h, q, d).start()

    def chunk(c):
        return pl.ds(c * DCH, DCH)

    def rsx(h, c, i):
        return remote(sb.at[h, slot(Z + zx(i)), chunk(c)], rx.at[h, slot(zx(i)), chunk(c)],
                      rx_s.at[h, c, i], rx_r.at[h, c, i], xnbr)

    def rsz(h, c, i):
        return remote(sb.at[h, slot(zx(i)), chunk(c)], zr.at[h, i - 1, :, chunk(c)],
                      rz_s.at[h, c, i - 1], rz_r.at[h, c, i - 1], zdev(i))

    def rsl(h, c):
        return remote(sb.at[h, slot(zx(3)), chunk(c)], rlin.at[h, :, chunk(c)],
                      rl_s.at[h, c], rl_r.at[h, c], zdev(1))

    def hspan(o):
        return pl.ds(pl.multiple_of(o * half, half), half)

    def down_early():
        def body(j, carry):
            cs = pl.ds(pl.multiple_of(j * DNC, DNC), DNC)
            pre[j] = jnp.dot(hid[:, hspan(d)], dw[hspan(d), cs], preferred_element_type=F32)
            return carry

        lax.fori_loop(0, EARLY * DCH // DNC, body, 0)

    def down(h, c):
        def body(j, carry):
            cs = pl.ds(pl.multiple_of(c * DCH + j * DNC, DNC), DNC)
            if c < EARLY:
                p = pre[c * (DCH // DNC) + j] + jnp.dot(
                    hid[:, hspan(1 - d)], dw[hspan(1 - d), cs], preferred_element_type=F32)
            else:
                p = jnp.dot(hid[...], dw[:, cs], preferred_element_type=F32)
            acc[h, :, cs] = p[:line]
            sb[h, line:, cs] = p[line:].astype(BF16)
            return carry

        lax.fori_loop(0, DCH // DNC, body, 0)
        for i in (3, 2, 1, 0):
            rsx(h, c, i).start()

    def merge(h, c, i):
        rsx(h, c, i).wait_recv()
        return acc[h, slot(zx(i)), chunk(c)] + rx[h, slot(zx(i)), chunk(c)].astype(F32)

    def direct(h, c):
        return (h, c) in DIRECT

    def rs_send(h, c):
        sb[h, slot(zx(3)), chunk(c)] = merge(h, c, 3).astype(BF16)
        if direct(h, c):
            rsz(h, c, 3).start()
        else:
            @pl.when(outer)
            def _():
                rsl(h, c).start()

            @pl.when(inner)
            def _():
                rsz(h, c, 3).start()

        total = merge(h, c, 2)
        if direct(h, c):
            sb[h, slot(zx(2)), chunk(c)] = total.astype(BF16)
            rsz(h, c, 2).start()
        else:
            @pl.when(outer)
            def _():
                sb[h, slot(zx(2)), chunk(c)] = total.astype(BF16)
                rsz(h, c, 2).start()

        sb[h, slot(zx(1)), chunk(c)] = merge(h, c, 1).astype(BF16)
        rsz(h, c, 1).start()

    def rs_relay(h, c):
        if direct(h, c):
            return

        @pl.when(inner)
        def _():
            rsl(h, c).wait_recv()
            total = acc[h, slot(zx(2)), chunk(c)] + rx[h, slot(zx(2)), chunk(c)].astype(F32)
            sb[h, slot(zx(2)), chunk(c)] = (total + rlin[h, :, chunk(c)].astype(F32)).astype(BF16)
            rsz(h, c, 2).start()

    def last(c):
        return remote(fin.at[:, chunk(c)], finrx.at[:, chunk(c)], fn_s.at[c], fn_r.at[c], peer)

    def rs_final(h, c):
        rsz(h, c, 1).wait_recv()
        rsz(h, c, 2).wait_recv()
        if direct(h, c):
            rsz(h, c, 3).wait_recv()
        else:
            @pl.when(inner)
            def _():
                rsz(h, c, 3).wait_recv()

        total = merge(h, c, 0)
        for i in range(3):
            total = total + zr[h, i, :, chunk(c)].astype(F32)
        result = total.astype(BF16)

        @pl.when(d == h)
        def _():
            out[:, pl.ds(pl.multiple_of(d * kl + c * DCH, DCH), DCH)] = result

        @pl.when(d != h)
        def _():
            fin[:, chunk(c)] = result
            last(c).start()

    def rs_drain(h):
        for c in range(chunks):
            for i in range(4):
                rsx(h, c, i).wait_send()
            rsz(h, c, 1).wait_send()
            rsz(h, c, 2).wait_send()
            if direct(h, c):
                rsz(h, c, 3).wait_send()
            else:
                @pl.when(outer)
                def _():
                    rsl(h, c).wait_send()

                @pl.when(inner)
                def _():
                    rsz(h, c, 3).wait_send()

    n0, n1 = len(AG0), len(AG1)
    for c in range(n0):
        ag_send(0, c)
    ago(0).start()
    age().start()
    ago(1).start()

    @pl.when(outer)
    def _():
        for h in range(2):
            for c in range(chunks):
                if not direct(h, c):
                    zr[h, 2, :, chunk(c)] = jnp.zeros((ROWS, DCH), BF16)

    for k in LOADS[:4]:
        prune(k)
    ag_forward(0, 0)
    ag_send(1, 0)
    for k in LOADS[4:6]:
        prune(k)
    ag_forward(0, 1)
    ag_send(1, 1)
    ag_edge_send()
    ago(0).wait_recv()
    ag_part(0)
    for q in range(groups):
        group(0, q, False, 0)
    for k in LOADS[6:8]:
        prune(k)
    for q in range(groups):
        group(0, q, True, 0)
    ag_finish(0)
    group(0, 0, False, 1)
    group(0, 1, False, 1)
    ag_forward(1, 0)
    for k in LOADS[8:10]:
        prune(k)
    group(0, 0, True, 1)
    hidden(0, 0)
    ag_forward(1, 1)
    ag_edge_forward()
    group(0, 1, True, 1)
    hidden(0, 1)
    for k in LOADS[10:]:
        prune(k)
    down_early()
    for q in range(groups):
        hd(0, q, 1 - d).wait_recv()
    for c in range(chunks):
        down(0, c)
    for q in range(groups):
        hd(0, q, d).wait_send()
    ag_finish(1)
    group(1, 0, False)
    group(1, 1, False)
    rs_send(0, 0)
    group(1, 0, True)
    rs_send(0, 1)
    rs_relay(0, 0)
    hidden(1, 0)
    group(1, 1, True)
    hidden(1, 1)
    rs_send(0, 2)
    rs_relay(0, 1)
    down_early()
    for q in range(groups):
        hd(1, q, 1 - d).wait_recv()
    down(1, 0)
    rs_send(0, 3)
    rs_relay(0, 2)
    down(1, 1)
    rs_relay(0, 3)
    down(1, 2)
    rs_send(1, 0)
    down(1, 3)
    for q in range(groups):
        hd(1, q, d).wait_send()
    for c in range(chunks):
        rs_final(0, c)
    rs_send(1, 1)
    rs_relay(1, 0)
    rs_send(1, 2)
    rs_relay(1, 1)
    rs_send(1, 3)
    for c in range(2, chunks):
        rs_relay(1, c)
    for c in range(chunks):
        rs_final(1, c)
    first.wait_send()
    ag_drain()
    rs_drain(0)
    rs_drain(1)
    for c in range(chunks):
        last(c).wait()
    out[:, cols(1 - d)] = finrx[...]


def fused(Z, tokens, ln_gain, gate_weight, up_weight, down_weight, gate_mask, up_mask, down_mask):
    kl, fl = gate_weight.shape
    dim = tokens.shape[1]
    half = fl // 2
    groups = half // GRP
    chunks = kl // DCH
    line = Z * ROWS
    m = 2 * line
    cuts = max(len(AG0), len(AG1))
    dma = pltpu.SemaphoreType.DMA
    vm = pl.BlockSpec(memory_space=pltpu.VMEM)
    hbm = pl.BlockSpec(memory_space=pl.ANY)
    flops = 2 * 2 * m * kl * fl * 3
    return pl.pallas_call(
        functools.partial(fused_kernel, Z),
        out_shape=jax.ShapeDtypeStruct((ROWS, dim), BF16),
        in_specs=[hbm] * 8,
        out_specs=vm,
        scratch_shapes=[
            pltpu.SMEM((kl // BLK, gate_mask.shape[1]), jnp.int32),
            pltpu.SMEM((kl // BLK, gate_mask.shape[1]), jnp.int32),
            pltpu.SMEM((kl // BLK, gate_mask.shape[1]), jnp.int32),
            pltpu.VMEM((ROWS, dim), BF16),
            pltpu.VMEM((1, dim), F32),
            pltpu.VMEM((2, kl, fl), BF16),
            pltpu.VMEM((fl, kl), BF16),
            pltpu.VMEM((ROWS, dim), BF16),
            pltpu.VMEM((2, m, kl), BF16),
            pltpu.VMEM((groups, 2, m, GRP), BF16),
            pltpu.VMEM((groups, 2, m, GRP), BF16),
            pltpu.VMEM((groups, 2, m, GRP), F32),
            pltpu.VMEM((2 * groups, m, GRP), F32),
            pltpu.VMEM((m, fl), BF16),
            pltpu.VMEM((2, m, kl), BF16),
            pltpu.VMEM((2, line, kl), F32),
            pltpu.VMEM((2, line, kl), BF16),
            pltpu.VMEM((2, ROWS, kl), BF16),
            pltpu.VMEM((2, 3, ROWS, kl), BF16),
            pltpu.VMEM((ROWS, kl), BF16),
            pltpu.VMEM((ROWS, kl), BF16),
            dma((5,)), dma((12,)),
            dma, dma,
            dma((2, cuts, 3)), dma((2, cuts, 3)), dma((2, cuts)),
            dma((2, cuts, 3)), dma((2, cuts, 3)),
            dma((2,)), dma((2,)),
            dma, dma, dma((2, 3)), dma((2, 3)), dma((2,)),
            dma((2, groups)), dma((2, groups)),
            dma((2, groups)), dma((2, groups)),
            dma((2, chunks, 4)), dma((2, chunks, 4)),
            dma((2, chunks, 3)), dma((2, chunks, 3)),
            dma((2, chunks)), dma((2, chunks)),
            dma((chunks,)), dma((chunks,)),
        ],
        compiler_params=pltpu.CompilerParams(
            collective_id=0, has_side_effects=True, vmem_limit_bytes=63 * 1024 * 1024
        ),
        cost_estimate=pl.CostEstimate(
            flops=flops, bytes_accessed=6 * kl * fl, transcendentals=0
        ),
    )(gate_mask, up_mask, down_mask.T, tokens, ln_gain.reshape(1, dim),
      gate_weight, up_weight, down_weight)


def solution(mesh):
    tensor = mesh.shape["tensor"]
    owners = mesh.shape["dp"]
    copies = mesh.shape["groups"]
    Z = tensor // 2

    def per_device(tokens, ln_gain, gate_weight, *rest):
        rows = tokens.shape[0]
        kl, fl = gate_weight.shape
        fits = (
            owners == 2 and tensor == 2 * Z and rows == ROWS and Z == 4
            and kl == 4 * DCH and fl == 4 * GRP
        )
        if fits:
            return fused(Z, tokens, ln_gain, gate_weight, *rest)
        return general(tokens, ln_gain, gate_weight, *rest)

    in_specs = (
        P(("groups", "dp", "tensor"), None),
        P(),
        P("dp", "tensor"),
        P("dp", "tensor"),
        P("tensor", "dp"),
        P(),
        P(),
        P(),
    )
    out_specs = P(("groups", "dp", "tensor"), None)
    return jax.shard_map(
        per_device, mesh=mesh, in_specs=in_specs, out_specs=out_specs, check_vma=False
    )
```

```python
import functools

import jax
import jax.numpy as jnp
from jax import lax
from jax.experimental import pallas as pl
from jax.experimental.pallas import tpu as pltpu
from jax.sharding import PartitionSpec as P

BLK = 128
ROWS = 16
DNC = 512
PW = 4
EARLY = 2
LOADS = (0, 4, 1, 5, 2, 6, 3, 7, 8, 9, 10, 11)
AG0 = (16, 16)
AG1 = (16, 8)
GRP = 512
DCH = 1024
EPSILON = 1e-05
F32 = jnp.float32
BF16 = jnp.bfloat16


def layer_norm(tokens, ln_gain):
    values = tokens.astype(F32)
    average = jnp.mean(values, axis=1, keepdims=True)
    centered = values - average
    variance = jnp.mean(centered * centered, axis=1, keepdims=True)
    return (centered * lax.rsqrt(variance + EPSILON) * ln_gain).astype(BF16)


def expand(mask, dtype):
    return jnp.repeat(jnp.repeat(mask.astype(dtype), BLK, axis=0), BLK, axis=1)


def general(tokens, ln_gain, gate_weight, up_weight, down_weight, gate_mask, up_mask, down_mask):
    t = lax.axis_index("tensor")
    d = lax.axis_index("dp")
    kl, fl = gate_weight.shape
    kb, fb = kl // BLK, fl // BLK
    normed = layer_norm(tokens, ln_gain)
    rows = lax.all_gather(normed, ("dp", "tensor"), axis=0, tiled=True)
    mine = lax.dynamic_slice_in_dim(rows, d * kl, kl, 1)

    def cut(mask, r0, c0, nr, nc):
        return expand(lax.dynamic_slice(mask, (r0, c0), (nr, nc)), BF16)

    gw = gate_weight * cut(gate_mask, d * kb, t * fb, kb, fb)
    uw = up_weight * cut(up_mask, d * kb, t * fb, kb, fb)
    dw = down_weight * cut(down_mask, t * fb, d * kb, fb, kb)
    gate = lax.psum(jnp.dot(mine, gw, preferred_element_type=F32), "dp")
    up = lax.psum(jnp.dot(mine, uw, preferred_element_type=F32), "dp")
    hidden = (jax.nn.silu(gate) * up).astype(BF16)
    part = jnp.dot(hidden, dw, preferred_element_type=F32)
    full = lax.all_gather(part, "dp", axis=1, tiled=True)
    half = full.shape[0] // lax.axis_size("dp")
    full = lax.dynamic_slice_in_dim(full, d * half, half, 0)
    return lax.psum_scatter(full, "tensor", scatter_dimension=0, tiled=True).astype(BF16)


def fused_kernel(
    Z,
    gm_hbm, um_hbm, dm_hbm, tok_hbm, gain_hbm, gw_hbm, uw_hbm, dw_hbm,
    out,
    gm, um, dmt, tok, gain,
    gu, dw, nrm, xbuf, exs, exr, own, pre, hid, sb, acc, rx, zr, fin, finrx,
    o_sem, w_sem, in_s, in_r, agz_s, agz_r, agl_s, agx_s, agx_r, ago_s, ago_r,
    ae_s, ae_r, aez_s, aez_r, ael_s, ex_s, ex_r, hd_s, hd_r,
    rx_s, rx_r, rz_s, rz_r, fn_s, fn_r,
):
    kl, fl = gu.shape[1:]
    half = fl // 2
    line = Z * ROWS
    groups = half // GRP
    chunks = kl // DCH
    d = lax.axis_index("dp")
    t = lax.axis_index("tensor")
    z = t // 2
    x = t % 2
    peer = {"dp": 1 - d}
    xnbr = {"tensor": z * 2 + (1 - x)}
    outer = jnp.logical_or(z == 0, z == Z - 1)
    inner = jnp.logical_not(outer)

    def zx(i):
        hi, lo = z // 2, z % 2
        if i & 2:
            hi = 1 - hi
        if i & 1:
            lo = 1 - lo
        return hi * 2 + lo

    def zdev(i):
        return {"tensor": zx(i) * 2 + x}

    def slot(j):
        return pl.ds(pl.multiple_of(j * ROWS, ROWS), ROWS)

    def remote(src, dst, ss, rs, dev):
        return pltpu.make_async_remote_copy(
            src_ref=src, dst_ref=dst, send_sem=ss, recv_sem=rs,
            device_id=dev, device_id_type=pl.DeviceIdType.MESH,
        )

    def wcopy(k):
        which, part = k // 4, k % 4
        src, dst = ((gw_hbm, gu.at[0]), (uw_hbm, gu.at[1]), (dw_hbm, dw))[which]
        n = src.shape[0] // 4
        return pltpu.make_async_copy(
            src.at[pl.ds(part * n, n), :], dst.at[pl.ds(part * n, n), :], w_sem.at[k]
        )

    barrier = pltpu.get_barrier_semaphore()

    def greet(dev):
        pl.semaphore_signal(barrier, inc=1, device_id=dev, device_id_type=pl.DeviceIdType.MESH)

    greet(peer)
    greet(xnbr)
    greet(zdev(1))
    greet(zdev(2))
    greet(zdev(3))
    for i in (1, 2, 3):
        greet({"dp": 1 - d, "tensor": zx(i) * 2 + x})

    kb = kl // BLK
    mine = pl.ds(pl.multiple_of(d * kb, kb), kb)
    small = [
        pltpu.make_async_copy(src, dst, o_sem.at[n])
        for n, (src, dst) in enumerate((
            (tok_hbm, tok), (gain_hbm, gain),
            (gm_hbm.at[mine, :], gm), (um_hbm.at[mine, :], um), (dm_hbm.at[mine, :], dmt),
        ))
    ]
    for copy in small:
        copy.start()
    small[0].wait()
    for copy in small[1:]:
        copy.wait()
    for k in LOADS:
        wcopy(k).start()

    values = tok[...].astype(F32)
    average = jnp.mean(values, axis=1, keepdims=True)
    centered = values - average
    variance = jnp.mean(centered * centered, axis=1, keepdims=True)
    nrm[...] = (centered * lax.rsqrt(variance + EPSILON) * gain[...]).astype(BF16)

    pl.semaphore_wait(barrier, 8)

    def cols(o):
        return pl.ds(pl.multiple_of(o * kl, kl), kl)

    first = remote(nrm.at[:, cols(1 - d)], xbuf.at[d, slot(z), :], in_s, in_r, peer)
    first.start()
    xbuf[d, slot(z), :] = nrm[:, cols(d)]
    remote(nrm.at[:, cols(d)], xbuf.at[1 - d, slot(z), :], in_s, in_r, peer).wait_recv()

    cuts = []
    for widths in (AG0, AG1):
        at, spans = 0, []
        for w in widths:
            spans.append(pl.ds(at * BLK, w * BLK))
            at += w
        cuts.append(spans)
    main1 = sum(AG1) * BLK
    ecols = pl.ds(main1, kl - main1)

    def agz(h, c, i):
        b = xbuf.at[h, slot(z), cuts[h][c]]
        return remote(b, b, agz_s.at[h, c, i - 1], agz_r.at[h, c, i - 1], zdev(i))

    def agz_in(h, c, i):
        b = xbuf.at[h, slot(zx(i)), cuts[h][c]]
        return remote(b, b, agz_s.at[h, c, i - 1], agz_r.at[h, c, i - 1], zdev(i))

    def agl(h, c):
        b = xbuf.at[h, slot(zx(2)), cuts[h][c]]
        return remote(b, b, agl_s.at[h, c], agz_r.at[h, c, 2], zdev(1))

    def agx(h, c, i):
        return remote(xbuf.at[h, slot(zx(i)), cuts[h][c]], xbuf.at[h, slot(Z + zx(i)), cuts[h][c]],
                      agx_s.at[h, c, i - 1], agx_r.at[h, c, i - 1], xnbr)

    def ago(h):
        span = pl.ds(0, main1 if h else kl)
        return remote(xbuf.at[h, slot(z), span], xbuf.at[h, slot(Z + z), span],
                      ago_s.at[h], ago_r.at[h], xnbr)

    def age():
        return remote(xbuf.at[1, slot(z), ecols], xbuf.at[1, slot(Z + z), ecols], ae_s, ae_r, xnbr)

    def aez(k, i):
        b = xbuf.at[1, slot(k * Z + z), ecols]
        return remote(b, b, aez_s.at[k, i - 1], aez_r.at[k, i - 1], zdev(i))

    def aez_in(k, i):
        b = xbuf.at[1, slot(k * Z + zx(i)), ecols]
        return remote(b, b, aez_s.at[k, i - 1], aez_r.at[k, i - 1], zdev(i))

    def ael(k):
        b = xbuf.at[1, slot(k * Z + zx(2)), ecols]
        return remote(b, b, ael_s.at[k], aez_r.at[k, 2], zdev(1))

    def ag_send(h, c):
        agz(h, c, 2).start()
        agz(h, c, 1).start()

        @pl.when(inner)
        def _():
            agz(h, c, 3).start()

    def ag_forward(h, c):
        agz_in(h, c, 2).wait_recv()

        @pl.when(inner)
        def _():
            agl(h, c).start()

        agx(h, c, 2).start()
        for i in (1, 3):
            agz_in(h, c, i).wait_recv()
            agx(h, c, i).start()

    def ag_edge_send():
        age().wait_recv()
        for k in range(2):
            aez(k, 2).start()
            aez(k, 1).start()

            @pl.when(inner)
            def _():
                aez(k, 3).start()

    def ag_edge_forward():
        for k in range(2):
            aez_in(k, 2).wait_recv()

            @pl.when(inner)
            def _():
                ael(k).start()

    def ag_part(c):
        for i in (1, 2, 3):
            agx(0, c, i).wait_recv()

    def ag_finish(h):
        if h:
            ago(h).wait_recv()
        for c in range(0 if h else 1, len(cuts[h])):
            for i in (1, 2, 3):
                agx(h, c, i).wait_recv()
        if h:
            for k in range(2):
                aez_in(k, 1).wait_recv()
                aez_in(k, 3).wait_recv()

    def ag_drain():
        age().wait_send()
        for k in range(2):
            aez(k, 1).wait_send()
            aez(k, 2).wait_send()

            @pl.when(inner)
            def _():
                aez(k, 3).wait_send()
                ael(k).wait_send()

        for h in range(2):
            ago(h).wait_send()
            for c in range(len(cuts[h])):
                for i in (1, 2, 3):
                    agx(h, c, i).wait_send()
                agz(h, c, 1).wait_send()
                agz(h, c, 2).wait_send()

                @pl.when(inner)
                def _():
                    agz(h, c, 3).wait_send()
                    agl(h, c).wait_send()

    def prune(k):
        wcopy(k).wait()
        which, part = k // 4, k % 4
        w = (gu.at[0], gu.at[1], dw)[which]
        nr, nc = w.shape[0] // BLK, w.shape[1] // BLK
        n = nr // 4

        def body(b, carry):
            rb = part * n + b
            rows = pl.ds(pl.multiple_of(rb * BLK, BLK), BLK)
            for c0 in range(0, nc, PW):
                keep = []
                for cb in range(c0, c0 + PW):
                    if which == 2:
                        bit = dmt[cb, t * nr + rb]
                    else:
                        bit = (gm, um)[which][rb, t * nc + cb]
                    keep.append(jnp.full((16, BLK), bit.astype(F32), F32).astype(BF16))
                keep = jnp.concatenate(keep, axis=1)
                cs = slice(c0 * BLK, (c0 + PW) * BLK)
                tile = w[rows, cs].reshape(BLK // 16, 16, PW * BLK)
                w[rows, cs] = (tile * keep[None]).reshape(BLK, PW * BLK)
            return carry

        lax.fori_loop(0, n, body, 0)

    def ex(h, q):
        return remote(exs.at[q], exr.at[q], ex_s.at[h, q], ex_r.at[h, q], peer)

    def group(h, q, mine, part=None):
        cs = pl.ds(pl.multiple_of((d if mine else 1 - d) * half + q * GRP, GRP), GRP)
        cut = AG0[0] * BLK
        ks = {None: pl.ds(0, kl), 0: pl.ds(0, cut), 1: pl.ds(cut, kl - cut)}[part]

        def body(m, carry):
            p = jnp.dot(xbuf[h, :, ks], gu[m, ks, cs], preferred_element_type=F32)
            if part == 1:
                p = p + (own[q, m] if mine else pre[q * 2 + m])
            if mine:
                own[q, m] = p
            elif part == 0:
                pre[q * 2 + m] = p
            else:
                exs[q, m] = p.astype(BF16)
            return carry

        lax.fori_loop(0, 2, body, 0)
        if not mine and part != 0:
            ex(h, q).start()

    def hcols(o, q):
        return pl.ds(pl.multiple_of(o * half + q * GRP, GRP), GRP)

    def hd(h, q, o):
        blk = hid.at[:, hcols(o, q)]
        return remote(blk, blk, hd_s.at[h, q], hd_r.at[h, q], peer)

    def hidden(h, q):
        ex(h, q).wait()
        g = own[q, 0] + exr[q, 0].astype(F32)
        u = own[q, 1] + exr[q, 1].astype(F32)
        hid[:, hcols(d, q)] = (g / (1.0 + jnp.exp(-g)) * u).astype(BF16)
        hd(h, q, d).start()

    def chunk(c):
        return pl.ds(c * DCH, DCH)

    def rsx(h, c, i):
        return remote(sb.at[h, slot(Z + zx(i)), chunk(c)], rx.at[h, slot(zx(i)), chunk(c)],
                      rx_s.at[h, c, i], rx_r.at[h, c, i], xnbr)

    def wide(o, c):
        return pl.ds(pl.multiple_of(o * kl + c * DCH, DCH), DCH)

    def rsz(h, c, i):
        return remote(sb.at[h, slot(zx(i)), chunk(c)], zr.at[i - 1, :, wide(d, c)],
                      rz_s.at[h, c, i - 1], rz_r.at[d, c, i - 1],
                      {"dp": h, "tensor": zx(i) * 2 + x})

    def rsz_in(o, c, i):
        return remote(sb.at[0, slot(zx(i)), chunk(c)], zr.at[i - 1, :, wide(o, c)],
                      rz_s.at[0, c, i - 1], rz_r.at[o, c, i - 1], zdev(i))

    def hspan(o):
        return pl.ds(pl.multiple_of(o * half, half), half)

    def down_early():
        def body(j, carry):
            cs = pl.ds(pl.multiple_of(j * DNC, DNC), DNC)
            pre[j] = jnp.dot(hid[:, hspan(d)], dw[hspan(d), cs], preferred_element_type=F32)
            return carry

        lax.fori_loop(0, EARLY * DCH // DNC, body, 0)

    def down(h, c):
        def body(j, carry):
            cs = pl.ds(pl.multiple_of(c * DCH + j * DNC, DNC), DNC)
            if c < EARLY:
                p = pre[c * (DCH // DNC) + j] + jnp.dot(
                    hid[:, hspan(1 - d)], dw[hspan(1 - d), cs], preferred_element_type=F32)
            else:
                p = jnp.dot(hid[...], dw[:, cs], preferred_element_type=F32)
            acc[h, :, cs] = p[:line]
            sb[h, line:, cs] = p[line:].astype(BF16)
            return carry

        lax.fori_loop(0, DCH // DNC, body, 0)
        for i in (3, 2, 1, 0):
            rsx(h, c, i).start()

    def merge(h, c, i):
        rsx(h, c, i).wait_recv()
        return acc[h, slot(zx(i)), chunk(c)] + rx[h, slot(zx(i)), chunk(c)].astype(F32)

    def rs_send(h, c):
        for i in (3, 2, 1):
            sb[h, slot(zx(i)), chunk(c)] = merge(h, c, i).astype(BF16)
            rsz(h, c, i).start()

    def share(c):
        return remote(fin.at[:, chunk(c)], finrx.at[:, chunk(c)], fn_s.at[c], fn_r.at[c], peer)

    def rs_own(h, c):
        total = merge(h, c, 0)

        @pl.when(d == h)
        def _():
            acc[h, slot(z), chunk(c)] = total

        @pl.when(d != h)
        def _():
            fin[:, chunk(c)] = total
            share(c).start()

    def rs_final(h):
        @pl.when(d == h)
        def _():
            for c in range(chunks):
                for o in range(2):
                    for i in (1, 2, 3):
                        rsz_in(o, c, i).wait_recv()
                share(c).wait_recv()
                mine = acc[h, slot(z), chunk(c)]
                other = finrx[:, chunk(c)]
                for i in range(3):
                    mine = mine + zr[i, :, wide(d, c)].astype(F32)
                    other = other + zr[i, :, wide(1 - d, c)].astype(F32)
                out[:, wide(d, c)] = mine.astype(BF16)
                out[:, wide(1 - d, c)] = other.astype(BF16)

    def rs_drain(h):
        for c in range(chunks):
            for i in range(4):
                rsx(h, c, i).wait_send()
            for i in (1, 2, 3):
                rsz(h, c, i).wait_send()

        @pl.when(d != h)
        def _():
            for c in range(chunks):
                share(c).wait_send()

    n0, n1 = len(AG0), len(AG1)
    for c in range(n0):
        ag_send(0, c)
    ago(0).start()
    age().start()
    ago(1).start()

    for k in LOADS[:4]:
        prune(k)
    ag_forward(0, 0)
    ag_send(1, 0)
    for k in LOADS[4:6]:
        prune(k)
    ag_forward(0, 1)
    ag_send(1, 1)
    ag_edge_send()
    ago(0).wait_recv()
    ag_part(0)
    for q in range(groups):
        group(0, q, False, 0)
    for k in LOADS[6:8]:
        prune(k)
    for q in range(groups):
        group(0, q, True, 0)
    ag_finish(0)
    group(0, 0, False, 1)
    group(0, 1, False, 1)
    ag_forward(1, 0)
    for k in LOADS[8:10]:
        prune(k)
    group(0, 0, True, 1)
    hidden(0, 0)
    ag_forward(1, 1)
    ag_edge_forward()
    group(0, 1, True, 1)
    hidden(0, 1)
    for k in LOADS[10:]:
        prune(k)
    down_early()
    for q in range(groups):
        hd(0, q, 1 - d).wait_recv()
    for c in range(chunks):
        down(0, c)
    for q in range(groups):
        hd(0, q, d).wait_send()
    ag_finish(1)
    group(1, 0, False)
    group(1, 1, False)
    rs_send(0, 0)
    group(1, 0, True)
    rs_send(0, 1)
    hidden(1, 0)
    group(1, 1, True)
    hidden(1, 1)
    rs_send(0, 2)
    down_early()
    for q in range(groups):
        hd(1, q, 1 - d).wait_recv()
    down(1, 0)
    rs_send(0, 3)
    down(1, 1)
    down(1, 2)
    rs_send(1, 0)
    down(1, 3)
    for q in range(groups):
        hd(1, q, d).wait_send()
    for c in range(chunks):
        rs_own(0, c)
    rs_send(1, 1)
    rs_send(1, 2)
    rs_own(1, 0)
    rs_own(1, 1)
    rs_send(1, 3)
    rs_own(1, 2)
    rs_own(1, 3)
    rs_final(0)
    rs_final(1)
    first.wait_send()
    ag_drain()
    rs_drain(0)
    rs_drain(1)


def fused(Z, tokens, ln_gain, gate_weight, up_weight, down_weight, gate_mask, up_mask, down_mask):
    kl, fl = gate_weight.shape
    dim = tokens.shape[1]
    half = fl // 2
    groups = half // GRP
    chunks = kl // DCH
    line = Z * ROWS
    m = 2 * line
    cuts = max(len(AG0), len(AG1))
    dma = pltpu.SemaphoreType.DMA
    vm = pl.BlockSpec(memory_space=pltpu.VMEM)
    hbm = pl.BlockSpec(memory_space=pl.ANY)
    flops = 2 * 2 * m * kl * fl * 3
    return pl.pallas_call(
        functools.partial(fused_kernel, Z),
        out_shape=jax.ShapeDtypeStruct((ROWS, dim), BF16),
        in_specs=[hbm] * 8,
        out_specs=vm,
        scratch_shapes=[
            pltpu.SMEM((kl // BLK, gate_mask.shape[1]), jnp.int32),
            pltpu.SMEM((kl // BLK, gate_mask.shape[1]), jnp.int32),
            pltpu.SMEM((kl // BLK, gate_mask.shape[1]), jnp.int32),
            pltpu.VMEM((ROWS, dim), BF16),
            pltpu.VMEM((1, dim), F32),
            pltpu.VMEM((2, kl, fl), BF16),
            pltpu.VMEM((fl, kl), BF16),
            pltpu.VMEM((ROWS, dim), BF16),
            pltpu.VMEM((2, m, kl), BF16),
            pltpu.VMEM((groups, 2, m, GRP), BF16),
            pltpu.VMEM((groups, 2, m, GRP), BF16),
            pltpu.VMEM((groups, 2, m, GRP), F32),
            pltpu.VMEM((2 * groups, m, GRP), F32),
            pltpu.VMEM((m, fl), BF16),
            pltpu.VMEM((2, m, kl), BF16),
            pltpu.VMEM((2, line, kl), F32),
            pltpu.VMEM((2, line, kl), BF16),
            pltpu.VMEM((3, ROWS, dim), BF16),
            pltpu.VMEM((ROWS, kl), F32),
            pltpu.VMEM((ROWS, kl), F32),
            dma((5,)), dma((12,)),
            dma, dma,
            dma((2, cuts, 3)), dma((2, cuts, 3)), dma((2, cuts)),
            dma((2, cuts, 3)), dma((2, cuts, 3)),
            dma((2,)), dma((2,)),
            dma, dma, dma((2, 3)), dma((2, 3)), dma((2,)),
            dma((2, groups)), dma((2, groups)),
            dma((2, groups)), dma((2, groups)),
            dma((2, chunks, 4)), dma((2, chunks, 4)),
            dma((2, chunks, 3)), dma((2, chunks, 3)),
            dma((chunks,)), dma((chunks,)),
        ],
        compiler_params=pltpu.CompilerParams(
            collective_id=0, has_side_effects=True, vmem_limit_bytes=63 * 1024 * 1024
        ),
        cost_estimate=pl.CostEstimate(
            flops=flops, bytes_accessed=6 * kl * fl, transcendentals=0
        ),
    )(gate_mask, up_mask, down_mask.T, tokens, ln_gain.reshape(1, dim),
      gate_weight, up_weight, down_weight)


def solution(mesh):
    tensor = mesh.shape["tensor"]
    owners = mesh.shape["dp"]
    copies = mesh.shape["groups"]
    Z = tensor // 2

    def per_device(tokens, ln_gain, gate_weight, *rest):
        rows = tokens.shape[0]
        kl, fl = gate_weight.shape
        fits = (
            owners == 2 and tensor == 2 * Z and rows == ROWS and Z == 4
            and kl == 4 * DCH and fl == 4 * GRP
        )
        if fits:
            return fused(Z, tokens, ln_gain, gate_weight, *rest)
        return general(tokens, ln_gain, gate_weight, *rest)

    in_specs = (
        P(("groups", "dp", "tensor"), None),
        P(),
        P("dp", "tensor"),
        P("dp", "tensor"),
        P("tensor", "dp"),
        P(),
        P(),
        P(),
    )
    out_specs = P(("groups", "dp", "tensor"), None)
    return jax.shard_map(
        per_device, mesh=mesh, in_specs=in_specs, out_specs=out_specs, check_vma=False
    )
```

```python
import functools

import jax
import jax.numpy as jnp
from jax import lax
from jax.experimental import pallas as pl
from jax.experimental.pallas import tpu as pltpu
from jax.sharding import PartitionSpec as P

BLK = 128
ROWS = 16
DNC = 512
PW = 4
EARLY = 2
LOADS = (0, 4, 1, 5, 2, 6, 3, 7, 8, 9, 10, 11)
AG0 = (16, 16)
AG1 = (16, 8)
GRP = 512
DCH = 1024
EPSILON = 1e-05
F32 = jnp.float32
BF16 = jnp.bfloat16


def layer_norm(tokens, ln_gain):
    values = tokens.astype(F32)
    average = jnp.mean(values, axis=1, keepdims=True)
    centered = values - average
    variance = jnp.mean(centered * centered, axis=1, keepdims=True)
    return (centered * lax.rsqrt(variance + EPSILON) * ln_gain).astype(BF16)


def expand(mask, dtype):
    return jnp.repeat(jnp.repeat(mask.astype(dtype), BLK, axis=0), BLK, axis=1)


def general(tokens, ln_gain, gate_weight, up_weight, down_weight, gate_mask, up_mask, down_mask):
    t = lax.axis_index("tensor")
    d = lax.axis_index("dp")
    kl, fl = gate_weight.shape
    kb, fb = kl // BLK, fl // BLK
    normed = layer_norm(tokens, ln_gain)
    rows = lax.all_gather(normed, ("dp", "tensor"), axis=0, tiled=True)
    mine = lax.dynamic_slice_in_dim(rows, d * kl, kl, 1)

    def cut(mask, r0, c0, nr, nc):
        return expand(lax.dynamic_slice(mask, (r0, c0), (nr, nc)), BF16)

    gw = gate_weight * cut(gate_mask, d * kb, t * fb, kb, fb)
    uw = up_weight * cut(up_mask, d * kb, t * fb, kb, fb)
    dw = down_weight * cut(down_mask, t * fb, d * kb, fb, kb)
    gate = lax.psum(jnp.dot(mine, gw, preferred_element_type=F32), "dp")
    up = lax.psum(jnp.dot(mine, uw, preferred_element_type=F32), "dp")
    hidden = (jax.nn.silu(gate) * up).astype(BF16)
    part = jnp.dot(hidden, dw, preferred_element_type=F32)
    full = lax.all_gather(part, "dp", axis=1, tiled=True)
    half = full.shape[0] // lax.axis_size("dp")
    full = lax.dynamic_slice_in_dim(full, d * half, half, 0)
    return lax.psum_scatter(full, "tensor", scatter_dimension=0, tiled=True).astype(BF16)


def fused_kernel(
    Z,
    gm_hbm, um_hbm, dm_hbm, tok_hbm, gain_hbm, gw_hbm, uw_hbm, dw_hbm,
    out,
    gm, um, dmt, tok, gain,
    gu, dw, nrm, xbuf, exs, exr, own, pre, hid, sb, acc, rx, zr, fin, finrx,
    o_sem, w_sem, in_s, in_r, agz_s, agz_r, agl_s, agx_s, agx_r, ago_s, ago_r,
    ae_s, ae_r, aez_s, aez_r, ael_s, ex_s, ex_r, hd_s, hd_r,
    rx_s, rx_r, rz_s, rz_r, fn_s, fn_r,
):
    kl, fl = gu.shape[1:]
    half = fl // 2
    line = Z * ROWS
    groups = half // GRP
    chunks = kl // DCH
    d = lax.axis_index("dp")
    t = lax.axis_index("tensor")
    z = t // 2
    x = t % 2
    peer = {"dp": 1 - d}
    xnbr = {"tensor": z * 2 + (1 - x)}
    outer = jnp.logical_or(z == 0, z == Z - 1)
    inner = jnp.logical_not(outer)

    def zx(i):
        hi, lo = z // 2, z % 2
        if i & 2:
            hi = 1 - hi
        if i & 1:
            lo = 1 - lo
        return hi * 2 + lo

    def zdev(i):
        return {"tensor": zx(i) * 2 + x}

    def slot(j):
        return pl.ds(pl.multiple_of(j * ROWS, ROWS), ROWS)

    def remote(src, dst, ss, rs, dev):
        return pltpu.make_async_remote_copy(
            src_ref=src, dst_ref=dst, send_sem=ss, recv_sem=rs,
            device_id=dev, device_id_type=pl.DeviceIdType.MESH,
        )

    def wcopy(k):
        which, part = k // 4, k % 4
        src, dst = ((gw_hbm, gu.at[0]), (uw_hbm, gu.at[1]), (dw_hbm, dw))[which]
        n = src.shape[0] // 4
        return pltpu.make_async_copy(
            src.at[pl.ds(part * n, n), :], dst.at[pl.ds(part * n, n), :], w_sem.at[k]
        )

    barrier = pltpu.get_barrier_semaphore()

    def greet(dev):
        pl.semaphore_signal(barrier, inc=1, device_id=dev, device_id_type=pl.DeviceIdType.MESH)

    greet(peer)
    greet(xnbr)
    greet(zdev(1))
    greet(zdev(2))
    greet(zdev(3))
    for i in (1, 2, 3):
        greet({"dp": 1 - d, "tensor": zx(i) * 2 + x})

    kb = kl // BLK
    mine = pl.ds(pl.multiple_of(d * kb, kb), kb)
    small = [
        pltpu.make_async_copy(src, dst, o_sem.at[n])
        for n, (src, dst) in enumerate((
            (tok_hbm, tok), (gain_hbm, gain),
            (gm_hbm.at[mine, :], gm), (um_hbm.at[mine, :], um), (dm_hbm.at[mine, :], dmt),
        ))
    ]
    for copy in small:
        copy.start()
    small[0].wait()
    for copy in small[1:]:
        copy.wait()
    for k in LOADS:
        wcopy(k).start()

    values = tok[...].astype(F32)
    average = jnp.mean(values, axis=1, keepdims=True)
    centered = values - average
    variance = jnp.mean(centered * centered, axis=1, keepdims=True)
    nrm[...] = (centered * lax.rsqrt(variance + EPSILON) * gain[...]).astype(BF16)

    pl.semaphore_wait(barrier, 8)

    def cols(o):
        return pl.ds(pl.multiple_of(o * kl, kl), kl)

    first = remote(nrm.at[:, cols(1 - d)], xbuf.at[d, slot(z), :], in_s, in_r, peer)
    first.start()
    xbuf[d, slot(z), :] = nrm[:, cols(d)]
    remote(nrm.at[:, cols(d)], xbuf.at[1 - d, slot(z), :], in_s, in_r, peer).wait_recv()

    cuts = []
    for widths in (AG0, AG1):
        at, spans = 0, []
        for w in widths:
            spans.append(pl.ds(at * BLK, w * BLK))
            at += w
        cuts.append(spans)
    main1 = sum(AG1) * BLK
    ecols = pl.ds(main1, kl - main1)

    def agz(h, c, i):
        b = xbuf.at[h, slot(z), cuts[h][c]]
        return remote(b, b, agz_s.at[h, c, i - 1], agz_r.at[h, c, i - 1], zdev(i))

    def agz_in(h, c, i):
        b = xbuf.at[h, slot(zx(i)), cuts[h][c]]
        return remote(b, b, agz_s.at[h, c, i - 1], agz_r.at[h, c, i - 1], zdev(i))

    def agl(h, c):
        b = xbuf.at[h, slot(zx(2)), cuts[h][c]]
        return remote(b, b, agl_s.at[h, c], agz_r.at[h, c, 2], zdev(1))

    def agx(h, c, i):
        return remote(xbuf.at[h, slot(zx(i)), cuts[h][c]], xbuf.at[h, slot(Z + zx(i)), cuts[h][c]],
                      agx_s.at[h, c, i - 1], agx_r.at[h, c, i - 1], xnbr)

    def ago(h):
        span = pl.ds(0, main1 if h else kl)
        return remote(xbuf.at[h, slot(z), span], xbuf.at[h, slot(Z + z), span],
                      ago_s.at[h], ago_r.at[h], xnbr)

    def age():
        return remote(xbuf.at[1, slot(z), ecols], xbuf.at[1, slot(Z + z), ecols], ae_s, ae_r, xnbr)

    def aez(k, i):
        b = xbuf.at[1, slot(k * Z + z), ecols]
        return remote(b, b, aez_s.at[k, i - 1], aez_r.at[k, i - 1], zdev(i))

    def aez_in(k, i):
        b = xbuf.at[1, slot(k * Z + zx(i)), ecols]
        return remote(b, b, aez_s.at[k, i - 1], aez_r.at[k, i - 1], zdev(i))

    def ael(k):
        b = xbuf.at[1, slot(k * Z + zx(2)), ecols]
        return remote(b, b, ael_s.at[k], aez_r.at[k, 2], zdev(1))

    def ag_send(h, c):
        agz(h, c, 2).start()
        agz(h, c, 1).start()

        @pl.when(inner)
        def _():
            agz(h, c, 3).start()

    def ag_forward(h, c):
        agz_in(h, c, 2).wait_recv()

        @pl.when(inner)
        def _():
            agl(h, c).start()

        agx(h, c, 2).start()
        for i in (1, 3):
            agz_in(h, c, i).wait_recv()
            agx(h, c, i).start()

    def ag_edge_send():
        age().wait_recv()
        for k in range(2):
            aez(k, 2).start()
            aez(k, 1).start()

            @pl.when(inner)
            def _():
                aez(k, 3).start()

    def ag_edge_forward():
        for k in range(2):
            aez_in(k, 2).wait_recv()

            @pl.when(inner)
            def _():
                ael(k).start()

    def ag_part(c):
        for i in (1, 2, 3):
            agx(0, c, i).wait_recv()

    def ag_finish(h):
        if h:
            ago(h).wait_recv()
        for c in range(0 if h else 1, len(cuts[h])):
            for i in (1, 2, 3):
                agx(h, c, i).wait_recv()
        if h:
            for k in range(2):
                aez_in(k, 1).wait_recv()
                aez_in(k, 3).wait_recv()

    def ag_drain():
        age().wait_send()
        for k in range(2):
            aez(k, 1).wait_send()
            aez(k, 2).wait_send()

            @pl.when(inner)
            def _():
                aez(k, 3).wait_send()
                ael(k).wait_send()

        for h in range(2):
            ago(h).wait_send()
            for c in range(len(cuts[h])):
                for i in (1, 2, 3):
                    agx(h, c, i).wait_send()
                agz(h, c, 1).wait_send()
                agz(h, c, 2).wait_send()

                @pl.when(inner)
                def _():
                    agz(h, c, 3).wait_send()
                    agl(h, c).wait_send()

    def prune(k):
        wcopy(k).wait()
        which, part = k // 4, k % 4
        w = (gu.at[0], gu.at[1], dw)[which]
        nr, nc = w.shape[0] // BLK, w.shape[1] // BLK
        n = nr // 4

        def body(b, carry):
            rb = part * n + b
            rows = pl.ds(pl.multiple_of(rb * BLK, BLK), BLK)
            for c0 in range(0, nc, PW):
                keep = []
                for cb in range(c0, c0 + PW):
                    if which == 2:
                        bit = dmt[cb, t * nr + rb]
                    else:
                        bit = (gm, um)[which][rb, t * nc + cb]
                    keep.append(jnp.full((16, BLK), bit.astype(F32), F32).astype(BF16))
                keep = jnp.concatenate(keep, axis=1)
                cs = slice(c0 * BLK, (c0 + PW) * BLK)
                tile = w[rows, cs].reshape(BLK // 16, 16, PW * BLK)
                w[rows, cs] = (tile * keep[None]).reshape(BLK, PW * BLK)
            return carry

        lax.fori_loop(0, n, body, 0)

    def ex(h, q):
        return remote(exs.at[q], exr.at[q], ex_s.at[h, q], ex_r.at[h, q], peer)

    def group(h, q, mine, part=None):
        cs = pl.ds(pl.multiple_of((d if mine else 1 - d) * half + q * GRP, GRP), GRP)
        cut = AG0[0] * BLK
        ks = {None: pl.ds(0, kl), 0: pl.ds(0, cut), 1: pl.ds(cut, kl - cut)}[part]

        def body(m, carry):
            p = jnp.dot(xbuf[h, :, ks], gu[m, ks, cs], preferred_element_type=F32)
            if part == 1:
                p = p + (own[q, m] if mine else pre[q * 2 + m])
            if mine:
                own[q, m] = p
            elif part == 0:
                pre[q * 2 + m] = p
            else:
                exs[q, m] = p.astype(BF16)
            return carry

        lax.fori_loop(0, 2, body, 0, unroll=True)
        if not mine and part != 0:
            ex(h, q).start()

    def hcols(o, q):
        return pl.ds(pl.multiple_of(o * half + q * GRP, GRP), GRP)

    def hd(h, q, o):
        blk = hid.at[:, hcols(o, q)]
        return remote(blk, blk, hd_s.at[h, q], hd_r.at[h, q], peer)

    def hidden(h, q):
        ex(h, q).wait()
        g = own[q, 0] + exr[q, 0].astype(F32)
        u = own[q, 1] + exr[q, 1].astype(F32)
        hid[:, hcols(d, q)] = (g / (1.0 + jnp.exp(-g)) * u).astype(BF16)
        hd(h, q, d).start()

    def chunk(c):
        return pl.ds(c * DCH, DCH)

    def rsx(h, c, i):
        return remote(sb.at[h, slot(Z + zx(i)), chunk(c)], rx.at[h, slot(zx(i)), chunk(c)],
                      rx_s.at[h, c, i], rx_r.at[h, c, i], xnbr)

    def wide(o, c):
        return pl.ds(pl.multiple_of(o * kl + c * DCH, DCH), DCH)

    def rsz(h, c, i):
        return remote(sb.at[h, slot(zx(i)), chunk(c)], zr.at[i - 1, :, wide(d, c)],
                      rz_s.at[h, c, i - 1], rz_r.at[d, c, i - 1],
                      {"dp": h, "tensor": zx(i) * 2 + x})

    def rsz_in(o, c, i):
        return remote(sb.at[0, slot(zx(i)), chunk(c)], zr.at[i - 1, :, wide(o, c)],
                      rz_s.at[0, c, i - 1], rz_r.at[o, c, i - 1], zdev(i))

    def hspan(o):
        return pl.ds(pl.multiple_of(o * half, half), half)

    def down_early():
        def body(j, carry):
            cs = pl.ds(pl.multiple_of(j * DNC, DNC), DNC)
            pre[j] = jnp.dot(hid[:, hspan(d)], dw[hspan(d), cs], preferred_element_type=F32)
            return carry

        lax.fori_loop(0, EARLY * DCH // DNC, body, 0, unroll=2)

    def down(h, c):
        def body(j, carry):
            cs = pl.ds(pl.multiple_of(c * DCH + j * DNC, DNC), DNC)
            if c < EARLY:
                p = pre[c * (DCH // DNC) + j] + jnp.dot(
                    hid[:, hspan(1 - d)], dw[hspan(1 - d), cs], preferred_element_type=F32)
            else:
                p = jnp.dot(hid[...], dw[:, cs], preferred_element_type=F32)
            acc[h, :, cs] = p[:line]
            sb[h, line:, cs] = p[line:].astype(BF16)
            return carry

        lax.fori_loop(0, DCH // DNC, body, 0, unroll=True)
        for i in (3, 2, 1, 0):
            rsx(h, c, i).start()

    def merge(h, c, i):
        rsx(h, c, i).wait_recv()
        return acc[h, slot(zx(i)), chunk(c)] + rx[h, slot(zx(i)), chunk(c)].astype(F32)

    def rs_send(h, c):
        for i in (3, 2, 1):
            sb[h, slot(zx(i)), chunk(c)] = merge(h, c, i).astype(BF16)
            rsz(h, c, i).start()

    def share(c):
        return remote(fin.at[:, chunk(c)], finrx.at[:, chunk(c)], fn_s.at[c], fn_r.at[c], peer)

    def rs_own(h, c):
        total = merge(h, c, 0)

        @pl.when(d == h)
        def _():
            acc[h, slot(z), chunk(c)] = total

        @pl.when(d != h)
        def _():
            fin[:, chunk(c)] = total
            share(c).start()

    def rs_final(h):
        @pl.when(d == h)
        def _():
            for c in range(chunks):
                for o in range(2):
                    for i in (1, 2, 3):
                        rsz_in(o, c, i).wait_recv()
                share(c).wait_recv()
                mine = acc[h, slot(z), chunk(c)]
                other = finrx[:, chunk(c)]
                for i in range(3):
                    mine = mine + zr[i, :, wide(d, c)].astype(F32)
                    other = other + zr[i, :, wide(1 - d, c)].astype(F32)
                out[:, wide(d, c)] = mine.astype(BF16)
                out[:, wide(1 - d, c)] = other.astype(BF16)

    def rs_drain(h):
        for c in range(chunks):
            for i in range(4):
                rsx(h, c, i).wait_send()
            for i in (1, 2, 3):
                rsz(h, c, i).wait_send()

        @pl.when(d != h)
        def _():
            for c in range(chunks):
                share(c).wait_send()

    n0, n1 = len(AG0), len(AG1)
    for c in range(n0):
        ag_send(0, c)
    ago(0).start()
    age().start()
    ago(1).start()

    for k in LOADS[:4]:
        prune(k)
    ag_forward(0, 0)
    ag_send(1, 0)
    for k in LOADS[4:6]:
        prune(k)
    ag_forward(0, 1)
    ag_send(1, 1)
    ag_edge_send()
    ago(0).wait_recv()
    ag_part(0)
    for q in range(groups):
        group(0, q, False, 0)
    for k in LOADS[6:8]:
        prune(k)
    for q in range(groups):
        group(0, q, True, 0)
    ag_finish(0)
    group(0, 0, False, 1)
    group(0, 1, False, 1)
    ag_forward(1, 0)
    for k in LOADS[8:10]:
        prune(k)
    group(0, 0, True, 1)
    hidden(0, 0)
    ag_forward(1, 1)
    ag_edge_forward()
    group(0, 1, True, 1)
    hidden(0, 1)
    for k in LOADS[10:]:
        prune(k)
    down_early()
    for q in range(groups):
        hd(0, q, 1 - d).wait_recv()
    for c in range(chunks):
        down(0, c)
    for q in range(groups):
        hd(0, q, d).wait_send()
    ag_finish(1)
    group(1, 0, False)
    group(1, 1, False)
    rs_send(0, 0)
    group(1, 0, True)
    rs_send(0, 1)
    hidden(1, 0)
    group(1, 1, True)
    hidden(1, 1)
    rs_send(0, 2)
    down_early()
    for q in range(groups):
        hd(1, q, 1 - d).wait_recv()
    down(1, 0)
    rs_send(0, 3)
    down(1, 1)
    down(1, 2)
    rs_send(1, 0)
    down(1, 3)
    for q in range(groups):
        hd(1, q, d).wait_send()
    for c in range(chunks):
        rs_own(0, c)
    rs_send(1, 1)
    rs_send(1, 2)
    rs_own(1, 0)
    rs_own(1, 1)
    rs_send(1, 3)
    rs_own(1, 2)
    rs_own(1, 3)
    rs_final(0)
    rs_final(1)
    first.wait_send()
    ag_drain()
    rs_drain(0)
    rs_drain(1)


def fused(Z, tokens, ln_gain, gate_weight, up_weight, down_weight, gate_mask, up_mask, down_mask):
    kl, fl = gate_weight.shape
    dim = tokens.shape[1]
    half = fl // 2
    groups = half // GRP
    chunks = kl // DCH
    line = Z * ROWS
    m = 2 * line
    cuts = max(len(AG0), len(AG1))
    dma = pltpu.SemaphoreType.DMA
    vm = pl.BlockSpec(memory_space=pltpu.VMEM)
    hbm = pl.BlockSpec(memory_space=pl.ANY)
    flops = 2 * 2 * m * kl * fl * 3
    return pl.pallas_call(
        functools.partial(fused_kernel, Z),
        out_shape=jax.ShapeDtypeStruct((ROWS, dim), BF16),
        in_specs=[hbm] * 8,
        out_specs=vm,
        scratch_shapes=[
            pltpu.SMEM((kl // BLK, gate_mask.shape[1]), jnp.int32),
            pltpu.SMEM((kl // BLK, gate_mask.shape[1]), jnp.int32),
            pltpu.SMEM((kl // BLK, gate_mask.shape[1]), jnp.int32),
            pltpu.VMEM((ROWS, dim), BF16),
            pltpu.VMEM((1, dim), F32),
            pltpu.VMEM((2, kl, fl), BF16),
            pltpu.VMEM((fl, kl), BF16),
            pltpu.VMEM((ROWS, dim), BF16),
            pltpu.VMEM((2, m, kl), BF16),
            pltpu.VMEM((groups, 2, m, GRP), BF16),
            pltpu.VMEM((groups, 2, m, GRP), BF16),
            pltpu.VMEM((groups, 2, m, GRP), F32),
            pltpu.VMEM((2 * groups, m, GRP), F32),
            pltpu.VMEM((m, fl), BF16),
            pltpu.VMEM((2, m, kl), BF16),
            pltpu.VMEM((2, line, kl), F32),
            pltpu.VMEM((2, line, kl), BF16),
            pltpu.VMEM((3, ROWS, dim), BF16),
            pltpu.VMEM((ROWS, kl), F32),
            pltpu.VMEM((ROWS, kl), F32),
            dma((5,)), dma((12,)),
            dma, dma,
            dma((2, cuts, 3)), dma((2, cuts, 3)), dma((2, cuts)),
            dma((2, cuts, 3)), dma((2, cuts, 3)),
            dma((2,)), dma((2,)),
            dma, dma, dma((2, 3)), dma((2, 3)), dma((2,)),
            dma((2, groups)), dma((2, groups)),
            dma((2, groups)), dma((2, groups)),
            dma((2, chunks, 4)), dma((2, chunks, 4)),
            dma((2, chunks, 3)), dma((2, chunks, 3)),
            dma((chunks,)), dma((chunks,)),
        ],
        compiler_params=pltpu.CompilerParams(
            collective_id=0, has_side_effects=True, vmem_limit_bytes=63 * 1024 * 1024
        ),
        cost_estimate=pl.CostEstimate(
            flops=flops, bytes_accessed=6 * kl * fl, transcendentals=0
        ),
    )(gate_mask, up_mask, down_mask.T, tokens, ln_gain.reshape(1, dim),
      gate_weight, up_weight, down_weight)


def solution(mesh):
    tensor = mesh.shape["tensor"]
    owners = mesh.shape["dp"]
    copies = mesh.shape["groups"]
    Z = tensor // 2

    def per_device(tokens, ln_gain, gate_weight, *rest):
        rows = tokens.shape[0]
        kl, fl = gate_weight.shape
        fits = (
            owners == 2 and tensor == 2 * Z and rows == ROWS and Z == 4
            and kl == 4 * DCH and fl == 4 * GRP
        )
        if fits:
            return fused(Z, tokens, ln_gain, gate_weight, *rest)
        return general(tokens, ln_gain, gate_weight, *rest)

    in_specs = (
        P(("groups", "dp", "tensor"), None),
        P(),
        P("dp", "tensor"),
        P("dp", "tensor"),
        P("tensor", "dp"),
        P(),
        P(),
        P(),
    )
    out_specs = P(("groups", "dp", "tensor"), None)
    return jax.shard_map(
        per_device, mesh=mesh, in_specs=in_specs, out_specs=out_specs, check_vma=False
    )
```

```python
import functools

import jax
import jax.numpy as jnp
from jax import lax
from jax.experimental import pallas as pl
from jax.experimental.pallas import tpu as pltpu
from jax.sharding import PartitionSpec as P

BLK = 128
ROWS = 16
DNC = 512
PW = 4
EARLY = 2
LOADS = (0, 4, 1, 5, 2, 6, 3, 7, 8, 9, 10, 11)
AG0 = (16, 16)
AG1 = (12, 12)
GRP = 512
DCH = 1024
EPSILON = 1e-05
F32 = jnp.float32
BF16 = jnp.bfloat16


def layer_norm(tokens, ln_gain):
    values = tokens.astype(F32)
    average = jnp.mean(values, axis=1, keepdims=True)
    centered = values - average
    variance = jnp.mean(centered * centered, axis=1, keepdims=True)
    return (centered * lax.rsqrt(variance + EPSILON) * ln_gain).astype(BF16)


def expand(mask, dtype):
    return jnp.repeat(jnp.repeat(mask.astype(dtype), BLK, axis=0), BLK, axis=1)


def general(tokens, ln_gain, gate_weight, up_weight, down_weight, gate_mask, up_mask, down_mask):
    t = lax.axis_index("tensor")
    d = lax.axis_index("dp")
    kl, fl = gate_weight.shape
    kb, fb = kl // BLK, fl // BLK
    normed = layer_norm(tokens, ln_gain)
    rows = lax.all_gather(normed, ("dp", "tensor"), axis=0, tiled=True)
    mine = lax.dynamic_slice_in_dim(rows, d * kl, kl, 1)

    def cut(mask, r0, c0, nr, nc):
        return expand(lax.dynamic_slice(mask, (r0, c0), (nr, nc)), BF16)

    gw = gate_weight * cut(gate_mask, d * kb, t * fb, kb, fb)
    uw = up_weight * cut(up_mask, d * kb, t * fb, kb, fb)
    dw = down_weight * cut(down_mask, t * fb, d * kb, fb, kb)
    gate = lax.psum(jnp.dot(mine, gw, preferred_element_type=F32), "dp")
    up = lax.psum(jnp.dot(mine, uw, preferred_element_type=F32), "dp")
    hidden = (jax.nn.silu(gate) * up).astype(BF16)
    part = jnp.dot(hidden, dw, preferred_element_type=F32)
    full = lax.all_gather(part, "dp", axis=1, tiled=True)
    half = full.shape[0] // lax.axis_size("dp")
    full = lax.dynamic_slice_in_dim(full, d * half, half, 0)
    return lax.psum_scatter(full, "tensor", scatter_dimension=0, tiled=True).astype(BF16)


def fused_kernel(
    Z,
    gm_hbm, um_hbm, dm_hbm, tok_hbm, gain_hbm, gw_hbm, uw_hbm, dw_hbm,
    out,
    gm, um, dmt, tok, gain,
    gu, dw, nrm, xbuf, exs, exr, own, pre, hid, sb, acc, rx, zr, fin, finrx,
    o_sem, w_sem, in_s, in_r, agz_s, agz_r, agl_s, agx_s, agx_r, ago_s, ago_r,
    ae_s, ae_r, aez_s, aez_r, ael_s, ex_s, ex_r, hd_s, hd_r,
    rx_s, rx_r, rz_s, rz_r, fn_s, fn_r,
):
    kl, fl = gu.shape[1:]
    half = fl // 2
    line = Z * ROWS
    groups = half // GRP
    chunks = kl // DCH
    d = lax.axis_index("dp")
    t = lax.axis_index("tensor")
    z = t // 2
    x = t % 2
    peer = {"dp": 1 - d}
    xnbr = {"tensor": z * 2 + (1 - x)}
    outer = jnp.logical_or(z == 0, z == Z - 1)
    inner = jnp.logical_not(outer)

    def zx(i):
        hi, lo = z // 2, z % 2
        if i & 2:
            hi = 1 - hi
        if i & 1:
            lo = 1 - lo
        return hi * 2 + lo

    def zdev(i):
        return {"tensor": zx(i) * 2 + x}

    def slot(j):
        return pl.ds(pl.multiple_of(j * ROWS, ROWS), ROWS)

    def remote(src, dst, ss, rs, dev):
        return pltpu.make_async_remote_copy(
            src_ref=src, dst_ref=dst, send_sem=ss, recv_sem=rs,
            device_id=dev, device_id_type=pl.DeviceIdType.MESH,
        )

    def wcopy(k):
        which, part = k // 4, k % 4
        src, dst = ((gw_hbm, gu.at[0]), (uw_hbm, gu.at[1]), (dw_hbm, dw))[which]
        n = src.shape[0] // 4
        return pltpu.make_async_copy(
            src.at[pl.ds(part * n, n), :], dst.at[pl.ds(part * n, n), :], w_sem.at[k]
        )

    barrier = pltpu.get_barrier_semaphore()

    def greet(dev):
        pl.semaphore_signal(barrier, inc=1, device_id=dev, device_id_type=pl.DeviceIdType.MESH)

    greet(peer)
    greet(xnbr)
    greet(zdev(1))
    greet(zdev(2))
    greet(zdev(3))
    for i in (1, 2, 3):
        greet({"dp": 1 - d, "tensor": zx(i) * 2 + x})

    kb = kl // BLK
    mine = pl.ds(pl.multiple_of(d * kb, kb), kb)
    small = [
        pltpu.make_async_copy(src, dst, o_sem.at[n])
        for n, (src, dst) in enumerate((
            (tok_hbm, tok), (gain_hbm, gain),
            (gm_hbm.at[mine, :], gm), (um_hbm.at[mine, :], um), (dm_hbm.at[mine, :], dmt),
        ))
    ]
    for copy in small:
        copy.start()
    small[0].wait()
    for copy in small[1:]:
        copy.wait()
    for k in LOADS:
        wcopy(k).start()

    values = tok[...].astype(F32)
    average = jnp.mean(values, axis=1, keepdims=True)
    centered = values - average
    variance = jnp.mean(centered * centered, axis=1, keepdims=True)
    nrm[...] = (centered * lax.rsqrt(variance + EPSILON) * gain[...]).astype(BF16)

    pl.semaphore_wait(barrier, 8)

    def cols(o):
        return pl.ds(pl.multiple_of(o * kl, kl), kl)

    first = remote(nrm.at[:, cols(1 - d)], xbuf.at[d, slot(z), :], in_s, in_r, peer)
    first.start()
    xbuf[d, slot(z), :] = nrm[:, cols(d)]
    remote(nrm.at[:, cols(d)], xbuf.at[1 - d, slot(z), :], in_s, in_r, peer).wait_recv()

    cuts = []
    for widths in (AG0, AG1):
        at, spans = 0, []
        for w in widths:
            spans.append(pl.ds(at * BLK, w * BLK))
            at += w
        cuts.append(spans)
    main1 = sum(AG1) * BLK
    ecols = pl.ds(main1, kl - main1)

    def agz(h, c, i):
        b = xbuf.at[h, slot(z), cuts[h][c]]
        return remote(b, b, agz_s.at[h, c, i - 1], agz_r.at[h, c, i - 1], zdev(i))

    def agz_in(h, c, i):
        b = xbuf.at[h, slot(zx(i)), cuts[h][c]]
        return remote(b, b, agz_s.at[h, c, i - 1], agz_r.at[h, c, i - 1], zdev(i))

    def agl(h, c):
        b = xbuf.at[h, slot(zx(2)), cuts[h][c]]
        return remote(b, b, agl_s.at[h, c], agz_r.at[h, c, 2], zdev(1))

    def agx(h, c, i):
        return remote(xbuf.at[h, slot(zx(i)), cuts[h][c]], xbuf.at[h, slot(Z + zx(i)), cuts[h][c]],
                      agx_s.at[h, c, i - 1], agx_r.at[h, c, i - 1], xnbr)

    def ago(h):
        span = pl.ds(0, main1 if h else kl)
        return remote(xbuf.at[h, slot(z), span], xbuf.at[h, slot(Z + z), span],
                      ago_s.at[h], ago_r.at[h], xnbr)

    def age():
        return remote(xbuf.at[1, slot(z), ecols], xbuf.at[1, slot(Z + z), ecols], ae_s, ae_r, xnbr)

    def aez(k, i):
        b = xbuf.at[1, slot(k * Z + z), ecols]
        return remote(b, b, aez_s.at[k, i - 1], aez_r.at[k, i - 1], zdev(i))

    def aez_in(k, i):
        b = xbuf.at[1, slot(k * Z + zx(i)), ecols]
        return remote(b, b, aez_s.at[k, i - 1], aez_r.at[k, i - 1], zdev(i))

    def ael(k):
        b = xbuf.at[1, slot(k * Z + zx(2)), ecols]
        return remote(b, b, ael_s.at[k], aez_r.at[k, 2], zdev(1))

    def ag_send(h, c):
        agz(h, c, 2).start()
        agz(h, c, 1).start()

        @pl.when(inner)
        def _():
            agz(h, c, 3).start()

    def ag_forward(h, c):
        agz_in(h, c, 2).wait_recv()

        @pl.when(inner)
        def _():
            agl(h, c).start()

        agx(h, c, 2).start()
        for i in (1, 3):
            agz_in(h, c, i).wait_recv()
            agx(h, c, i).start()

    def ag_edge_send():
        age().wait_recv()
        for k in range(2):
            aez(k, 2).start()
            aez(k, 1).start()

            @pl.when(inner)
            def _():
                aez(k, 3).start()

    def ag_edge_forward():
        for k in range(2):
            aez_in(k, 2).wait_recv()

            @pl.when(inner)
            def _():
                ael(k).start()

    def ag_part(c):
        for i in (1, 2, 3):
            agx(0, c, i).wait_recv()

    def ag_finish(h):
        if h:
            ago(h).wait_recv()
        for c in range(0 if h else 1, len(cuts[h])):
            for i in (1, 2, 3):
                agx(h, c, i).wait_recv()
        if h:
            for k in range(2):
                aez_in(k, 1).wait_recv()
                aez_in(k, 3).wait_recv()

    def ag_drain():
        age().wait_send()
        for k in range(2):
            aez(k, 1).wait_send()
            aez(k, 2).wait_send()

            @pl.when(inner)
            def _():
                aez(k, 3).wait_send()
                ael(k).wait_send()

        for h in range(2):
            ago(h).wait_send()
            for c in range(len(cuts[h])):
                for i in (1, 2, 3):
                    agx(h, c, i).wait_send()
                agz(h, c, 1).wait_send()
                agz(h, c, 2).wait_send()

                @pl.when(inner)
                def _():
                    agz(h, c, 3).wait_send()
                    agl(h, c).wait_send()

    def prune(k):
        wcopy(k).wait()
        which, part = k // 4, k % 4
        w = (gu.at[0], gu.at[1], dw)[which]
        nr, nc = w.shape[0] // BLK, w.shape[1] // BLK
        n = nr // 4

        def body(b, carry):
            rb = part * n + b
            rows = pl.ds(pl.multiple_of(rb * BLK, BLK), BLK)
            for c0 in range(0, nc, PW):
                keep = []
                for cb in range(c0, c0 + PW):
                    if which == 2:
                        bit = dmt[cb, t * nr + rb]
                    else:
                        bit = (gm, um)[which][rb, t * nc + cb]
                    keep.append(jnp.full((16, BLK), bit.astype(F32), F32).astype(BF16))
                keep = jnp.concatenate(keep, axis=1)
                cs = slice(c0 * BLK, (c0 + PW) * BLK)
                tile = w[rows, cs].reshape(BLK // 16, 16, PW * BLK)
                w[rows, cs] = (tile * keep[None]).reshape(BLK, PW * BLK)
            return carry

        lax.fori_loop(0, n, body, 0)

    def ex(h, q):
        return remote(exs.at[q], exr.at[q], ex_s.at[h, q], ex_r.at[h, q], peer)

    def group(h, q, mine, part=None):
        cs = pl.ds(pl.multiple_of((d if mine else 1 - d) * half + q * GRP, GRP), GRP)
        cut = AG0[0] * BLK
        ks = {None: pl.ds(0, kl), 0: pl.ds(0, cut), 1: pl.ds(cut, kl - cut)}[part]

        def body(m, carry):
            p = jnp.dot(xbuf[h, :, ks], gu[m, ks, cs], preferred_element_type=F32)
            if part == 1:
                p = p + (own[q, m] if mine else pre[q * 2 + m])
            if mine:
                own[q, m] = p
            elif part == 0:
                pre[q * 2 + m] = p
            else:
                exs[q, m] = p.astype(BF16)
            return carry

        lax.fori_loop(0, 2, body, 0, unroll=True)
        if not mine and part != 0:
            ex(h, q).start()

    def hcols(o, q):
        return pl.ds(pl.multiple_of(o * half + q * GRP, GRP), GRP)

    def hd(h, q, o):
        blk = hid.at[:, hcols(o, q)]
        return remote(blk, blk, hd_s.at[h, q], hd_r.at[h, q], peer)

    def hidden(h, q):
        ex(h, q).wait()
        g = own[q, 0] + exr[q, 0].astype(F32)
        u = own[q, 1] + exr[q, 1].astype(F32)
        hid[:, hcols(d, q)] = (g / (1.0 + jnp.exp(-g)) * u).astype(BF16)
        hd(h, q, d).start()

    def chunk(c):
        return pl.ds(c * DCH, DCH)

    def rsx(h, c, i):
        return remote(sb.at[h, slot(Z + zx(i)), chunk(c)], rx.at[h, slot(zx(i)), chunk(c)],
                      rx_s.at[h, c, i], rx_r.at[h, c, i], xnbr)

    def wide(o, c):
        return pl.ds(pl.multiple_of(o * kl + c * DCH, DCH), DCH)

    def rsz(h, c, i):
        return remote(sb.at[h, slot(zx(i)), chunk(c)], zr.at[i - 1, :, wide(d, c)],
                      rz_s.at[h, c, i - 1], rz_r.at[d, c, i - 1],
                      {"dp": h, "tensor": zx(i) * 2 + x})

    def rsz_in(o, c, i):
        return remote(sb.at[0, slot(zx(i)), chunk(c)], zr.at[i - 1, :, wide(o, c)],
                      rz_s.at[0, c, i - 1], rz_r.at[o, c, i - 1], zdev(i))

    def hspan(o):
        return pl.ds(pl.multiple_of(o * half, half), half)

    def down_early():
        def body(j, carry):
            cs = pl.ds(pl.multiple_of(j * DNC, DNC), DNC)
            pre[j] = jnp.dot(hid[:, hspan(d)], dw[hspan(d), cs], preferred_element_type=F32)
            return carry

        lax.fori_loop(0, EARLY * DCH // DNC, body, 0, unroll=2)

    def down(h, c):
        def body(j, carry):
            cs = pl.ds(pl.multiple_of(c * DCH + j * DNC, DNC), DNC)
            if c < EARLY:
                p = pre[c * (DCH // DNC) + j] + jnp.dot(
                    hid[:, hspan(1 - d)], dw[hspan(1 - d), cs], preferred_element_type=F32)
            else:
                p = jnp.dot(hid[...], dw[:, cs], preferred_element_type=F32)
            acc[h, :, cs] = p[:line]
            sb[h, line:, cs] = p[line:].astype(BF16)
            return carry

        lax.fori_loop(0, DCH // DNC, body, 0, unroll=True)
        for i in (3, 2, 1, 0):
            rsx(h, c, i).start()

    def merge(h, c, i):
        rsx(h, c, i).wait_recv()
        return acc[h, slot(zx(i)), chunk(c)] + rx[h, slot(zx(i)), chunk(c)].astype(F32)

    def rs_send(h, c):
        for i in (3, 2, 1):
            sb[h, slot(zx(i)), chunk(c)] = merge(h, c, i).astype(BF16)
            rsz(h, c, i).start()

    def share(c):
        return remote(fin.at[:, chunk(c)], finrx.at[:, chunk(c)], fn_s.at[c], fn_r.at[c], peer)

    def rs_own(h, c):
        total = merge(h, c, 0)

        @pl.when(d == h)
        def _():
            acc[h, slot(z), chunk(c)] = total

        @pl.when(d != h)
        def _():
            fin[:, chunk(c)] = total
            share(c).start()

    def rs_final(h):
        @pl.when(d == h)
        def _():
            for c in range(chunks):
                for o in range(2):
                    for i in (1, 2, 3):
                        rsz_in(o, c, i).wait_recv()
                share(c).wait_recv()
                mine = acc[h, slot(z), chunk(c)]
                other = finrx[:, chunk(c)]
                for i in range(3):
                    mine = mine + zr[i, :, wide(d, c)].astype(F32)
                    other = other + zr[i, :, wide(1 - d, c)].astype(F32)
                out[:, wide(d, c)] = mine.astype(BF16)
                out[:, wide(1 - d, c)] = other.astype(BF16)

    def rs_drain(h):
        for c in range(chunks):
            for i in range(4):
                rsx(h, c, i).wait_send()
            for i in (1, 2, 3):
                rsz(h, c, i).wait_send()

        @pl.when(d != h)
        def _():
            for c in range(chunks):
                share(c).wait_send()

    n0, n1 = len(AG0), len(AG1)
    for c in range(n0):
        ag_send(0, c)
    ago(0).start()
    age().start()
    ago(1).start()

    for k in LOADS[:4]:
        prune(k)
    ag_forward(0, 0)
    ag_send(1, 0)
    for k in LOADS[4:6]:
        prune(k)
    ag_forward(0, 1)
    ag_send(1, 1)
    ag_edge_send()
    ago(0).wait_recv()
    ag_part(0)
    for q in range(groups):
        group(0, q, False, 0)
    for k in LOADS[6:8]:
        prune(k)
    for q in range(groups):
        group(0, q, True, 0)
    ag_finish(0)
    group(0, 0, False, 1)
    ag_forward(1, 0)
    group(0, 1, False, 1)
    for k in LOADS[8:10]:
        prune(k)
    group(0, 0, True, 1)
    hidden(0, 0)
    ag_forward(1, 1)
    ag_edge_forward()
    group(0, 1, True, 1)
    hidden(0, 1)
    for k in LOADS[10:]:
        prune(k)
    down_early()
    for q in range(groups):
        hd(0, q, 1 - d).wait_recv()
    for c in range(chunks):
        down(0, c)
    for q in range(groups):
        hd(0, q, d).wait_send()
    ag_finish(1)
    group(1, 0, False)
    group(1, 1, False)
    rs_send(0, 0)
    group(1, 0, True)
    rs_send(0, 1)
    hidden(1, 0)
    group(1, 1, True)
    hidden(1, 1)
    rs_send(0, 2)
    down_early()
    for q in range(groups):
        hd(1, q, 1 - d).wait_recv()
    down(1, 0)
    rs_send(0, 3)
    down(1, 1)
    down(1, 2)
    rs_send(1, 0)
    down(1, 3)
    for q in range(groups):
        hd(1, q, d).wait_send()
    first.wait_send()
    ag_drain()
    for c in range(chunks):
        rs_own(0, c)
    rs_send(1, 1)
    rs_send(1, 2)
    rs_own(1, 0)
    rs_own(1, 1)
    rs_send(1, 3)
    rs_own(1, 2)
    rs_own(1, 3)
    rs_drain(0)
    rs_final(0)
    rs_drain(1)
    rs_final(1)


def fused(Z, tokens, ln_gain, gate_weight, up_weight, down_weight, gate_mask, up_mask, down_mask):
    kl, fl = gate_weight.shape
    dim = tokens.shape[1]
    half = fl // 2
    groups = half // GRP
    chunks = kl // DCH
    line = Z * ROWS
    m = 2 * line
    cuts = max(len(AG0), len(AG1))
    dma = pltpu.SemaphoreType.DMA
    vm = pl.BlockSpec(memory_space=pltpu.VMEM)
    hbm = pl.BlockSpec(memory_space=pl.ANY)
    flops = 2 * 2 * m * kl * fl * 3
    return pl.pallas_call(
        functools.partial(fused_kernel, Z),
        out_shape=jax.ShapeDtypeStruct((ROWS, dim), BF16),
        in_specs=[hbm] * 8,
        out_specs=vm,
        scratch_shapes=[
            pltpu.SMEM((kl // BLK, gate_mask.shape[1]), jnp.int32),
            pltpu.SMEM((kl // BLK, gate_mask.shape[1]), jnp.int32),
            pltpu.SMEM((kl // BLK, gate_mask.shape[1]), jnp.int32),
            pltpu.VMEM((ROWS, dim), BF16),
            pltpu.VMEM((1, dim), F32),
            pltpu.VMEM((2, kl, fl), BF16),
            pltpu.VMEM((fl, kl), BF16),
            pltpu.VMEM((ROWS, dim), BF16),
            pltpu.VMEM((2, m, kl), BF16),
            pltpu.VMEM((groups, 2, m, GRP), BF16),
            pltpu.VMEM((groups, 2, m, GRP), BF16),
            pltpu.VMEM((groups, 2, m, GRP), F32),
            pltpu.VMEM((2 * groups, m, GRP), F32),
            pltpu.VMEM((m, fl), BF16),
            pltpu.VMEM((2, m, kl), BF16),
            pltpu.VMEM((2, line, kl), F32),
            pltpu.VMEM((2, line, kl), BF16),
            pltpu.VMEM((3, ROWS, dim), BF16),
            pltpu.VMEM((ROWS, kl), F32),
            pltpu.VMEM((ROWS, kl), F32),
            dma((5,)), dma((12,)),
            dma, dma,
            dma((2, cuts, 3)), dma((2, cuts, 3)), dma((2, cuts)),
            dma((2, cuts, 3)), dma((2, cuts, 3)),
            dma((2,)), dma((2,)),
            dma, dma, dma((2, 3)), dma((2, 3)), dma((2,)),
            dma((2, groups)), dma((2, groups)),
            dma((2, groups)), dma((2, groups)),
            dma((2, chunks, 4)), dma((2, chunks, 4)),
            dma((2, chunks, 3)), dma((2, chunks, 3)),
            dma((chunks,)), dma((chunks,)),
        ],
        compiler_params=pltpu.CompilerParams(
            collective_id=0, has_side_effects=True, vmem_limit_bytes=63 * 1024 * 1024
        ),
        cost_estimate=pl.CostEstimate(
            flops=flops, bytes_accessed=6 * kl * fl, transcendentals=0
        ),
    )(gate_mask, up_mask, down_mask.T, tokens, ln_gain.reshape(1, dim),
      gate_weight, up_weight, down_weight)


def solution(mesh):
    tensor = mesh.shape["tensor"]
    owners = mesh.shape["dp"]
    copies = mesh.shape["groups"]
    Z = tensor // 2

    def per_device(tokens, ln_gain, gate_weight, *rest):
        rows = tokens.shape[0]
        kl, fl = gate_weight.shape
        fits = (
            owners == 2 and tensor == 2 * Z and rows == ROWS and Z == 4
            and kl == 4 * DCH and fl == 4 * GRP
        )
        if fits:
            return fused(Z, tokens, ln_gain, gate_weight, *rest)
        return general(tokens, ln_gain, gate_weight, *rest)

    in_specs = (
        P(("groups", "dp", "tensor"), None),
        P(),
        P("dp", "tensor"),
        P("dp", "tensor"),
        P("tensor", "dp"),
        P(),
        P(),
        P(),
    )
    out_specs = P(("groups", "dp", "tensor"), None)
    return jax.shard_map(
        per_device, mesh=mesh, in_specs=in_specs, out_specs=out_specs, check_vma=False
    )
```

```python
import functools

import jax
import jax.numpy as jnp
from jax import lax
from jax.experimental import pallas as pl
from jax.experimental.pallas import tpu as pltpu
from jax.sharding import PartitionSpec as P

BLK = 128
ROWS = 16
DNC = 512
PW = 4
EARLY = 2
LOADS = (0, 4, 1, 5, 2, 6, 3, 7, 8, 9, 10, 11)
AG0 = (16, 16)
AG1 = (12, 12)
GRP = 512
DCH = 1024
EPSILON = 1e-05
F32 = jnp.float32
BF16 = jnp.bfloat16


def layer_norm(tokens, ln_gain):
    values = tokens.astype(F32)
    average = jnp.mean(values, axis=1, keepdims=True)
    centered = values - average
    variance = jnp.mean(centered * centered, axis=1, keepdims=True)
    return (centered * lax.rsqrt(variance + EPSILON) * ln_gain).astype(BF16)


def expand(mask, dtype):
    return jnp.repeat(jnp.repeat(mask.astype(dtype), BLK, axis=0), BLK, axis=1)


def general(tokens, ln_gain, gate_weight, up_weight, down_weight, gate_mask, up_mask, down_mask):
    t = lax.axis_index("tensor")
    d = lax.axis_index("dp")
    kl, fl = gate_weight.shape
    kb, fb = kl // BLK, fl // BLK
    normed = layer_norm(tokens, ln_gain)
    rows = lax.all_gather(normed, ("dp", "tensor"), axis=0, tiled=True)
    mine = lax.dynamic_slice_in_dim(rows, d * kl, kl, 1)

    def cut(mask, r0, c0, nr, nc):
        return expand(lax.dynamic_slice(mask, (r0, c0), (nr, nc)), BF16)

    gw = gate_weight * cut(gate_mask, d * kb, t * fb, kb, fb)
    uw = up_weight * cut(up_mask, d * kb, t * fb, kb, fb)
    dw = down_weight * cut(down_mask, t * fb, d * kb, fb, kb)
    gate = lax.psum(jnp.dot(mine, gw, preferred_element_type=F32), "dp")
    up = lax.psum(jnp.dot(mine, uw, preferred_element_type=F32), "dp")
    hidden = (jax.nn.silu(gate) * up).astype(BF16)
    part = jnp.dot(hidden, dw, preferred_element_type=F32)
    full = lax.all_gather(part, "dp", axis=1, tiled=True)
    half = full.shape[0] // lax.axis_size("dp")
    full = lax.dynamic_slice_in_dim(full, d * half, half, 0)
    return lax.psum_scatter(full, "tensor", scatter_dimension=0, tiled=True).astype(BF16)


def fused_kernel(
    Z,
    gm_hbm, um_hbm, dm_hbm, tok_hbm, gain_hbm, gw_hbm, uw_hbm, dw_hbm,
    out,
    gm, um, dmt, tok, gain,
    gu, dw, nrm, xbuf, exs, exr, own, pre, hid, sb, acc, rx, zr, fin, finrx,
    o_sem, w_sem, in_s, in_r, agz_s, agz_r, agl_s, agx_s, agx_r, ago_s, ago_r,
    ae_s, ae_r, aez_s, aez_r, ael_s, ex_s, ex_r, hd_s, hd_r,
    rx_s, rx_r, rz_s, rz_r, fn_s, fn_r,
):
    kl, fl = gu.shape[1:]
    half = fl // 2
    line = Z * ROWS
    groups = half // GRP
    chunks = kl // DCH
    d = lax.axis_index("dp")
    t = lax.axis_index("tensor")
    z = t // 2
    x = t % 2
    peer = {"dp": 1 - d}
    xnbr = {"tensor": z * 2 + (1 - x)}
    outer = jnp.logical_or(z == 0, z == Z - 1)
    inner = jnp.logical_not(outer)

    def zx(i):
        hi, lo = z // 2, z % 2
        if i & 2:
            hi = 1 - hi
        if i & 1:
            lo = 1 - lo
        return hi * 2 + lo

    def zdev(i):
        return {"tensor": zx(i) * 2 + x}

    def slot(j):
        return pl.ds(pl.multiple_of(j * ROWS, ROWS), ROWS)

    def remote(src, dst, ss, rs, dev):
        return pltpu.make_async_remote_copy(
            src_ref=src, dst_ref=dst, send_sem=ss, recv_sem=rs,
            device_id=dev, device_id_type=pl.DeviceIdType.MESH,
        )

    def wcopy(k):
        which, part = k // 4, k % 4
        src, dst = ((gw_hbm, gu.at[0]), (uw_hbm, gu.at[1]), (dw_hbm, dw))[which]
        n = src.shape[0] // 4
        return pltpu.make_async_copy(
            src.at[pl.ds(part * n, n), :], dst.at[pl.ds(part * n, n), :], w_sem.at[k]
        )

    barrier = pltpu.get_barrier_semaphore()

    def greet(dev):
        pl.semaphore_signal(barrier, inc=1, device_id=dev, device_id_type=pl.DeviceIdType.MESH)

    for i in (3, 2, 1):
        greet(zdev(i))
        greet({"dp": 1 - d, "tensor": zx(i) * 2 + x})
    greet(xnbr)
    greet(peer)

    kb = kl // BLK
    mine = pl.ds(pl.multiple_of(d * kb, kb), kb)
    small = [
        pltpu.make_async_copy(src, dst, o_sem.at[n])
        for n, (src, dst) in enumerate((
            (tok_hbm, tok), (gain_hbm, gain),
            (gm_hbm.at[mine, :], gm), (um_hbm.at[mine, :], um), (dm_hbm.at[mine, :], dmt),
        ))
    ]
    for copy in small:
        copy.start()
    small[0].wait()
    for copy in small[1:]:
        copy.wait()
    for k in LOADS:
        wcopy(k).start()

    values = tok[...].astype(F32)
    average = jnp.mean(values, axis=1, keepdims=True)
    centered = values - average
    variance = jnp.mean(centered * centered, axis=1, keepdims=True)
    nrm[...] = (centered * lax.rsqrt(variance + EPSILON) * gain[...]).astype(BF16)

    pl.semaphore_wait(barrier, 8)

    def cols(o):
        return pl.ds(pl.multiple_of(o * kl, kl), kl)

    first = remote(nrm.at[:, cols(1 - d)], xbuf.at[d, slot(z), :], in_s, in_r, peer)
    first.start()
    xbuf[d, slot(z), :] = nrm[:, cols(d)]
    remote(nrm.at[:, cols(d)], xbuf.at[1 - d, slot(z), :], in_s, in_r, peer).wait_recv()

    cuts = []
    for widths in (AG0, AG1):
        at, spans = 0, []
        for w in widths:
            spans.append(pl.ds(at * BLK, w * BLK))
            at += w
        cuts.append(spans)
    main1 = sum(AG1) * BLK
    ecols = pl.ds(main1, kl - main1)

    def agz(h, c, i):
        b = xbuf.at[h, slot(z), cuts[h][c]]
        return remote(b, b, agz_s.at[h, c, i - 1], agz_r.at[h, c, i - 1], zdev(i))

    def agz_in(h, c, i):
        b = xbuf.at[h, slot(zx(i)), cuts[h][c]]
        return remote(b, b, agz_s.at[h, c, i - 1], agz_r.at[h, c, i - 1], zdev(i))

    def agl(h, c):
        b = xbuf.at[h, slot(zx(2)), cuts[h][c]]
        return remote(b, b, agl_s.at[h, c], agz_r.at[h, c, 2], zdev(1))

    def agx(h, c, i):
        return remote(xbuf.at[h, slot(zx(i)), cuts[h][c]], xbuf.at[h, slot(Z + zx(i)), cuts[h][c]],
                      agx_s.at[h, c, i - 1], agx_r.at[h, c, i - 1], xnbr)

    def ago(h):
        span = pl.ds(0, main1 if h else kl)
        return remote(xbuf.at[h, slot(z), span], xbuf.at[h, slot(Z + z), span],
                      ago_s.at[h], ago_r.at[h], xnbr)

    def age():
        return remote(xbuf.at[1, slot(z), ecols], xbuf.at[1, slot(Z + z), ecols], ae_s, ae_r, xnbr)

    def aez(k, i):
        b = xbuf.at[1, slot(k * Z + z), ecols]
        return remote(b, b, aez_s.at[k, i - 1], aez_r.at[k, i - 1], zdev(i))

    def aez_in(k, i):
        b = xbuf.at[1, slot(k * Z + zx(i)), ecols]
        return remote(b, b, aez_s.at[k, i - 1], aez_r.at[k, i - 1], zdev(i))

    def ael(k):
        b = xbuf.at[1, slot(k * Z + zx(2)), ecols]
        return remote(b, b, ael_s.at[k], aez_r.at[k, 2], zdev(1))

    def ag_send(h, c):
        agz(h, c, 2).start()
        agz(h, c, 1).start()

        @pl.when(inner)
        def _():
            agz(h, c, 3).start()

    def ag_forward(h, c):
        agz_in(h, c, 2).wait_recv()

        @pl.when(inner)
        def _():
            agl(h, c).start()

        agx(h, c, 2).start()
        for i in (1, 3):
            agz_in(h, c, i).wait_recv()
            agx(h, c, i).start()

    def ag_edge_send():
        age().wait_recv()
        for k in range(2):
            aez(k, 2).start()
            aez(k, 1).start()

            @pl.when(inner)
            def _():
                aez(k, 3).start()

    def ag_edge_forward():
        for k in range(2):
            aez_in(k, 2).wait_recv()

            @pl.when(inner)
            def _():
                ael(k).start()

    def ag_part(c):
        for i in (1, 2, 3):
            agx(0, c, i).wait_recv()

    def ag_finish(h):
        if h:
            ago(h).wait_recv()
        for c in range(0 if h else 1, len(cuts[h])):
            for i in (1, 2, 3):
                agx(h, c, i).wait_recv()
        if h:
            for k in range(2):
                aez_in(k, 1).wait_recv()
                aez_in(k, 3).wait_recv()

    def ag_drain():
        age().wait_send()
        for k in range(2):
            aez(k, 1).wait_send()
            aez(k, 2).wait_send()

            @pl.when(inner)
            def _():
                aez(k, 3).wait_send()
                ael(k).wait_send()

        for h in range(2):
            ago(h).wait_send()
            for c in range(len(cuts[h])):
                for i in (1, 2, 3):
                    agx(h, c, i).wait_send()
                agz(h, c, 1).wait_send()
                agz(h, c, 2).wait_send()

                @pl.when(inner)
                def _():
                    agz(h, c, 3).wait_send()
                    agl(h, c).wait_send()

    def prune(k):
        wcopy(k).wait()
        which, part = k // 4, k % 4
        w = (gu.at[0], gu.at[1], dw)[which]
        nr, nc = w.shape[0] // BLK, w.shape[1] // BLK
        n = nr // 4

        def body(b, carry):
            rb = part * n + b
            rows = pl.ds(pl.multiple_of(rb * BLK, BLK), BLK)
            for c0 in range(0, nc, PW):
                keep = []
                for cb in range(c0, c0 + PW):
                    if which == 2:
                        bit = dmt[cb, t * nr + rb]
                    else:
                        bit = (gm, um)[which][rb, t * nc + cb]
                    keep.append(jnp.full((16, BLK), bit.astype(F32), F32).astype(BF16))
                keep = jnp.concatenate(keep, axis=1)
                cs = slice(c0 * BLK, (c0 + PW) * BLK)
                tile = w[rows, cs].reshape(BLK // 16, 16, PW * BLK)
                w[rows, cs] = (tile * keep[None]).reshape(BLK, PW * BLK)
            return carry

        lax.fori_loop(0, n, body, 0)

    def ex(h, q):
        return remote(exs.at[q], exr.at[q], ex_s.at[h, q], ex_r.at[h, q], peer)

    def group(h, q, mine, part=None):
        cs = pl.ds(pl.multiple_of((d if mine else 1 - d) * half + q * GRP, GRP), GRP)
        cut = AG0[0] * BLK
        ks = {None: pl.ds(0, kl), 0: pl.ds(0, cut), 1: pl.ds(cut, kl - cut)}[part]

        def body(m, carry):
            p = jnp.dot(xbuf[h, :, ks], gu[m, ks, cs], preferred_element_type=F32)
            if part == 1:
                p = p + (own[q, m] if mine else pre[q * 2 + m])
            if mine:
                own[q, m] = p
            elif part == 0:
                pre[q * 2 + m] = p
            else:
                exs[q, m] = p.astype(BF16)
            return carry

        lax.fori_loop(0, 2, body, 0, unroll=True)
        if not mine and part != 0:
            ex(h, q).start()

    def hcols(o, q):
        return pl.ds(pl.multiple_of(o * half + q * GRP, GRP), GRP)

    def hd(h, q, o):
        blk = hid.at[:, hcols(o, q)]
        return remote(blk, blk, hd_s.at[h, q], hd_r.at[h, q], peer)

    def hidden(h, q):
        ex(h, q).wait()
        g = own[q, 0] + exr[q, 0].astype(F32)
        u = own[q, 1] + exr[q, 1].astype(F32)
        hid[:, hcols(d, q)] = (g / (1.0 + jnp.exp(-g)) * u).astype(BF16)
        hd(h, q, d).start()

    def chunk(c):
        return pl.ds(c * DCH, DCH)

    def rsx(h, c, i):
        return remote(sb.at[h, slot(Z + zx(i)), chunk(c)], rx.at[h, slot(zx(i)), chunk(c)],
                      rx_s.at[h, c, i], rx_r.at[h, c, i], xnbr)

    def wide(o, c):
        return pl.ds(pl.multiple_of(o * kl + c * DCH, DCH), DCH)

    def rsz(h, c, i):
        return remote(sb.at[h, slot(zx(i)), chunk(c)], zr.at[i - 1, :, wide(d, c)],
                      rz_s.at[h, c, i - 1], rz_r.at[d, c, i - 1],
                      {"dp": h, "tensor": zx(i) * 2 + x})

    def rsz_in(o, c, i):
        return remote(sb.at[0, slot(zx(i)), chunk(c)], zr.at[i - 1, :, wide(o, c)],
                      rz_s.at[0, c, i - 1], rz_r.at[o, c, i - 1], zdev(i))

    def hspan(o):
        return pl.ds(pl.multiple_of(o * half, half), half)

    def down_early():
        def body(j, carry):
            cs = pl.ds(pl.multiple_of(j * DNC, DNC), DNC)
            pre[j] = jnp.dot(hid[:, hspan(d)], dw[hspan(d), cs], preferred_element_type=F32)
            return carry

        lax.fori_loop(0, EARLY * DCH // DNC, body, 0, unroll=2)

    def down(h, c):
        def body(j, carry):
            cs = pl.ds(pl.multiple_of(c * DCH + j * DNC, DNC), DNC)
            if c < EARLY:
                p = pre[c * (DCH // DNC) + j] + jnp.dot(
                    hid[:, hspan(1 - d)], dw[hspan(1 - d), cs], preferred_element_type=F32)
            else:
                p = jnp.dot(hid[...], dw[:, cs], preferred_element_type=F32)
            acc[h, :, cs] = p[:line]
            sb[h, line:, cs] = p[line:].astype(BF16)
            return carry

        lax.fori_loop(0, DCH // DNC, body, 0, unroll=True)
        for i in (3, 2, 1, 0):
            rsx(h, c, i).start()

    def merge(h, c, i):
        rsx(h, c, i).wait_recv()
        return acc[h, slot(zx(i)), chunk(c)] + rx[h, slot(zx(i)), chunk(c)].astype(F32)

    def rs_send(h, c):
        for i in (3, 2, 1):
            sb[h, slot(zx(i)), chunk(c)] = merge(h, c, i).astype(BF16)
            rsz(h, c, i).start()

    def share(c):
        return remote(fin.at[:, chunk(c)], finrx.at[:, chunk(c)], fn_s.at[c], fn_r.at[c], peer)

    def rs_own(h, c):
        total = merge(h, c, 0)

        @pl.when(d == h)
        def _():
            acc[h, slot(z), chunk(c)] = total

        @pl.when(d != h)
        def _():
            fin[:, chunk(c)] = total
            share(c).start()

    def rs_final(h):
        @pl.when(d == h)
        def _():
            for c in range(chunks):
                for o in range(2):
                    for i in (1, 2, 3):
                        rsz_in(o, c, i).wait_recv()
                share(c).wait_recv()
                mine = acc[h, slot(z), chunk(c)]
                other = finrx[:, chunk(c)]
                for i in range(3):
                    mine = mine + zr[i, :, wide(d, c)].astype(F32)
                    other = other + zr[i, :, wide(1 - d, c)].astype(F32)
                out[:, wide(d, c)] = mine.astype(BF16)
                out[:, wide(1 - d, c)] = other.astype(BF16)

    def rs_drain(h):
        for c in range(chunks):
            for i in range(4):
                rsx(h, c, i).wait_send()
            for i in (1, 2, 3):
                rsz(h, c, i).wait_send()

        @pl.when(d != h)
        def _():
            for c in range(chunks):
                share(c).wait_send()

    n0, n1 = len(AG0), len(AG1)
    for c in range(n0):
        ag_send(0, c)
    ago(0).start()
    age().start()
    ago(1).start()

    for k in LOADS[:4]:
        prune(k)
    ag_forward(0, 0)
    ag_send(1, 0)
    for k in LOADS[4:6]:
        prune(k)
    ag_forward(0, 1)
    ag_send(1, 1)
    ag_edge_send()
    ago(0).wait_recv()
    ag_part(0)
    for q in range(groups):
        group(0, q, False, 0)
    for k in LOADS[6:8]:
        prune(k)
    for q in range(groups):
        group(0, q, True, 0)
    ag_finish(0)
    group(0, 0, False, 1)
    ag_forward(1, 0)
    group(0, 1, False, 1)
    for k in LOADS[8:10]:
        prune(k)
    group(0, 0, True, 1)
    hidden(0, 0)
    ag_forward(1, 1)
    ag_edge_forward()
    group(0, 1, True, 1)
    hidden(0, 1)
    for k in LOADS[10:]:
        prune(k)
    down_early()
    for q in range(groups):
        hd(0, q, 1 - d).wait_recv()
    for c in range(chunks):
        down(0, c)
    for q in range(groups):
        hd(0, q, d).wait_send()
    ag_finish(1)
    group(1, 0, False)
    group(1, 1, False)
    rs_send(0, 0)
    group(1, 0, True)
    rs_send(0, 1)
    hidden(1, 0)
    group(1, 1, True)
    hidden(1, 1)
    rs_send(0, 2)
    down_early()
    for q in range(groups):
        hd(1, q, 1 - d).wait_recv()
    down(1, 0)
    rs_send(0, 3)
    down(1, 1)
    down(1, 2)
    rs_send(1, 0)
    down(1, 3)
    for q in range(groups):
        hd(1, q, d).wait_send()
    first.wait_send()
    ag_drain()
    for c in range(chunks):
        rs_own(0, c)
    rs_send(1, 1)
    rs_send(1, 2)
    rs_own(1, 0)
    rs_own(1, 1)
    rs_send(1, 3)
    rs_own(1, 2)
    rs_own(1, 3)
    rs_drain(0)
    rs_final(0)
    rs_drain(1)
    rs_final(1)


def fused(Z, tokens, ln_gain, gate_weight, up_weight, down_weight, gate_mask, up_mask, down_mask):
    kl, fl = gate_weight.shape
    dim = tokens.shape[1]
    half = fl // 2
    groups = half // GRP
    chunks = kl // DCH
    line = Z * ROWS
    m = 2 * line
    cuts = max(len(AG0), len(AG1))
    dma = pltpu.SemaphoreType.DMA
    vm = pl.BlockSpec(memory_space=pltpu.VMEM)
    hbm = pl.BlockSpec(memory_space=pl.ANY)
    flops = 2 * 2 * m * kl * fl * 3
    return pl.pallas_call(
        functools.partial(fused_kernel, Z),
        out_shape=jax.ShapeDtypeStruct((ROWS, dim), BF16),
        in_specs=[hbm] * 8,
        out_specs=vm,
        scratch_shapes=[
            pltpu.SMEM((kl // BLK, gate_mask.shape[1]), jnp.int32),
            pltpu.SMEM((kl // BLK, gate_mask.shape[1]), jnp.int32),
            pltpu.SMEM((kl // BLK, gate_mask.shape[1]), jnp.int32),
            pltpu.VMEM((ROWS, dim), BF16),
            pltpu.VMEM((1, dim), F32),
            pltpu.VMEM((2, kl, fl), BF16),
            pltpu.VMEM((fl, kl), BF16),
            pltpu.VMEM((ROWS, dim), BF16),
            pltpu.VMEM((2, m, kl), BF16),
            pltpu.VMEM((groups, 2, m, GRP), BF16),
            pltpu.VMEM((groups, 2, m, GRP), BF16),
            pltpu.VMEM((groups, 2, m, GRP), F32),
            pltpu.VMEM((2 * groups, m, GRP), F32),
            pltpu.VMEM((m, fl), BF16),
            pltpu.VMEM((2, m, kl), BF16),
            pltpu.VMEM((2, line, kl), F32),
            pltpu.VMEM((2, line, kl), BF16),
            pltpu.VMEM((3, ROWS, dim), BF16),
            pltpu.VMEM((ROWS, kl), F32),
            pltpu.VMEM((ROWS, kl), F32),
            dma((5,)), dma((12,)),
            dma, dma,
            dma((2, cuts, 3)), dma((2, cuts, 3)), dma((2, cuts)),
            dma((2, cuts, 3)), dma((2, cuts, 3)),
            dma((2,)), dma((2,)),
            dma, dma, dma((2, 3)), dma((2, 3)), dma((2,)),
            dma((2, groups)), dma((2, groups)),
            dma((2, groups)), dma((2, groups)),
            dma((2, chunks, 4)), dma((2, chunks, 4)),
            dma((2, chunks, 3)), dma((2, chunks, 3)),
            dma((chunks,)), dma((chunks,)),
        ],
        compiler_params=pltpu.CompilerParams(
            collective_id=0, has_side_effects=True, vmem_limit_bytes=63 * 1024 * 1024
        ),
        cost_estimate=pl.CostEstimate(
            flops=flops, bytes_accessed=6 * kl * fl, transcendentals=0
        ),
    )(gate_mask, up_mask, down_mask.T, tokens, ln_gain.reshape(1, dim),
      gate_weight, up_weight, down_weight)


def solution(mesh):
    tensor = mesh.shape["tensor"]
    owners = mesh.shape["dp"]
    copies = mesh.shape["groups"]
    Z = tensor // 2

    def per_device(tokens, ln_gain, gate_weight, *rest):
        rows = tokens.shape[0]
        kl, fl = gate_weight.shape
        fits = (
            owners == 2 and tensor == 2 * Z and rows == ROWS and Z == 4
            and kl == 4 * DCH and fl == 4 * GRP
        )
        if fits:
            return fused(Z, tokens, ln_gain, gate_weight, *rest)
        return general(tokens, ln_gain, gate_weight, *rest)

    in_specs = (
        P(("groups", "dp", "tensor"), None),
        P(),
        P("dp", "tensor"),
        P("dp", "tensor"),
        P("tensor", "dp"),
        P(),
        P(),
        P(),
    )
    out_specs = P(("groups", "dp", "tensor"), None)
    return jax.shard_map(
        per_device, mesh=mesh, in_specs=in_specs, out_specs=out_specs, check_vma=False
    )
```
